32 devices in a mesh: row: 4 (over y, x), col: 8 (over z, core).
Axes of the slice: x: 2, y: 2, z: 4, core: 2. Of those that a mesh axis runs over, the one named last changes fastest.
Arguments:
- latent: bfloat16 [128, 256, 512], P('row', 'col'), may hold values from -12 to 12
- conv_scale: float32 [512], replicated, may hold values from 0.5 to 1.5
- conv_shift: float32 [512], replicated, may hold values from -3 to 3
- expand_weight: bfloat16 [512, 2048], replicated, may hold values from -0.25 to 0.25
- depth_kernel: float32 [9, 2048], replicated, may hold values from -2 to 2
- squeeze_down: bfloat16 [2048, 128], replicated, may hold values from -0.5 to 0.5
- squeeze_up: bfloat16 [128, 2048], replicated, may hold values from -0.5 to 0.5
- project_weight: bfloat16 [2048, 512], replicated, may hold values from -0.125 to 0.125
- block_gain: float32 [512], replicated, may hold values from 0.5 to 1.5
- block_projection: bfloat16 [512, 1536], replicated, may hold values from -0.25 to 0.25
- block_output: bfloat16 [512, 512], replicated, may hold values from -0.25 to 0.25
- block_table: float32 [16, 225], replicated, may hold values from -4 to 300
- first_gain: float32 [512], replicated, may hold values from 0.5 to 1.5
- first_expand: bfloat16 [512, 2048], replicated, may hold values from -0.25 to 0.25
- first_reduce: bfloat16 [2048, 512], replicated, may hold values from -0.125 to 0.125
- grid_gain: float32 [512], replicated, may hold values from 0.5 to 1.5
- grid_projection: bfloat16 [512, 1536], replicated, may hold values from -0.25 to 0.25
- grid_output: bfloat16 [512, 512], replicated, may hold values from -0.25 to 0.25
- grid_table: float32 [16, 225], replicated, may hold values from -4 to 300
- second_gain: float32 [512], replicated, may hold values from 0.5 to 1.5
- second_expand: bfloat16 [512, 2048], replicated, may hold values from -0.25 to 0.25
- second_reduce: bfloat16 [2048, 512], replicated, may hold values from -0.125 to 0.125
Outputs:
- nowcast_latent: bfloat16 [128, 256, 512], P('row', 'col')
The draws below stay inside these ranges and needn't reach their ends.
All inputs are finite; a program needn't handle non-finite values.
Results may differ from the reference program's by a relative error of at most 0.012.
Values may be sent and summed in bfloat16 or wider, within the bound.
A program may use at most 128 MiB of HBM per device.

```python
import jax
import jax.numpy as jnp
from jax import lax

C = 512
HEADS = 16
E = 2048
FF = 2048
SQUEEZE = 128
WIN = 8
HEIGHT = 128
WIDTH = 256
N_ROW = 4
N_COL = 8


def draw_latent(key, part):
    key = jax.random.fold_in(key, 7301)
    row_key = jax.random.fold_in(key, 0)
    col_key = jax.random.fold_in(key, 1)
    main_key = jax.random.fold_in(key, 2)
    offset_key = jax.random.fold_in(key, 4)
    patch_key = jax.random.fold_in(key, 5)
    rising = 3.0 ** (jnp.arange(HEIGHT, dtype=jnp.float32) / max(HEIGHT - 1, 1))
    row_factor = rising * jnp.exp(jax.random.uniform(row_key, (HEIGHT,), jnp.float32, -0.35, 0.35))
    col_factor = jnp.exp(jax.random.uniform(col_key, (WIDTH,), jnp.float32, -0.35, 0.35))
    base = jnp.clip(jax.random.normal(main_key, (HEIGHT, WIDTH, C), jnp.float32), -4.0, 4.0)
    centre_key, across_key, tall_key, broad_key = jax.random.split(patch_key, 4)
    centre_row = jax.random.uniform(centre_key, (4,), jnp.float32, 0.0, 1.0)
    centre_col = jax.random.uniform(across_key, (4,), jnp.float32, 0.05, 0.95)
    half_row = jax.random.uniform(tall_key, (4,), jnp.float32, 0.2, 0.45)
    half_col = jax.random.uniform(broad_key, (4,), jnp.float32, 0.06, 0.12)
    row_spot = (jnp.arange(HEIGHT, dtype=jnp.float32) + 0.5) / HEIGHT
    col_spot = (jnp.arange(WIDTH, dtype=jnp.float32) + 0.5) / WIDTH
    storm = jnp.zeros((HEIGHT, WIDTH), jnp.float32)
    for patch in range(4):
        row_inside = jax.nn.sigmoid((half_row[patch] - jnp.abs(row_spot - centre_row[patch])) / 0.02)
        col_inside = jax.nn.sigmoid((half_col[patch] - jnp.abs(col_spot - centre_col[patch])) / 0.01)
        storm = storm + row_inside[:, None] * col_inside[None, :]
    storm = jnp.clip(storm, 0.0, 1.0)
    channel_offset = jax.random.uniform(offset_key, (C,), jnp.float32, -2.5, 2.5)
    shaped = base * row_factor[:, None, None] * col_factor[None, :, None] / 1.7 * (1.0 + 0.5 * storm[:, :, None])
    shaped = shaped + (2.0 * storm - 1.0)[:, :, None] * channel_offset
    return jnp.clip(shaped, -12.0, 12.0).astype(jnp.bfloat16)


def relative_table(key, salt):
    key = jax.random.fold_in(key, salt)
    base_key = jax.random.fold_in(key, 0)
    spots = (2 * WIN - 1) ** 2
    base = jnp.clip(jax.random.normal(base_key, (HEADS, spots), jnp.float32), -4.0, 4.0)
    return base.astype(jnp.float32)


def draw_block_table(key, part):
    return relative_table(key, 8101)


def draw_grid_table(key, part):
    return relative_table(key, 8209)


def noise(rng, shape, deviation, bound, kind=jnp.bfloat16):
    return jnp.clip(deviation * jax.random.normal(rng, shape, jnp.float32), -bound, bound).astype(kind)


def setup_inputs(seed: int = 0) -> dict:
    streams_of = jax.random.split(jax.random.key(seed), 23)
    return {
        "latent": draw_latent(jax.random.fold_in(streams_of[22], 71), 0),
        "conv_scale": jnp.clip(1.0 + 0.1 * jax.random.normal(streams_of[1], (C,), jnp.float32), 0.5, 1.5),
        "conv_shift": noise(streams_of[2], (C,), 0.5, 3.0, jnp.float32),
        "expand_weight": noise(streams_of[3], (C, E), C ** -0.5, 0.25),
        "depth_kernel": noise(streams_of[4], (9, E), 9 ** -0.5, 2.0, jnp.float32),
        "squeeze_down": noise(streams_of[5], (E, SQUEEZE), SQUEEZE ** -0.5, 0.5),
        "squeeze_up": noise(streams_of[6], (SQUEEZE, E), SQUEEZE ** -0.5, 0.5),
        "project_weight": noise(streams_of[7], (E, C), E ** -0.5, 0.125),
        "block_gain": jnp.clip(1.0 + 0.1 * jax.random.normal(streams_of[8], (C,), jnp.float32), 0.5, 1.5),
        "block_projection": noise(streams_of[9], (C, 3 * C), C ** -0.5, 0.25),
        "block_output": noise(streams_of[10], (C, C), C ** -0.5, 0.25),
        "block_table": draw_block_table(jax.random.fold_in(streams_of[22], 71), 0),
        "first_gain": jnp.clip(1.0 + 0.1 * jax.random.normal(streams_of[12], (C,), jnp.float32), 0.5, 1.5),
        "first_expand": noise(streams_of[13], (C, FF), C ** -0.5, 0.25),
        "first_reduce": noise(streams_of[14], (FF, C), FF ** -0.5, 0.125),
        "grid_gain": jnp.clip(1.0 + 0.1 * jax.random.normal(streams_of[15], (C,), jnp.float32), 0.5, 1.5),
        "grid_projection": noise(streams_of[16], (C, 3 * C), C ** -0.5, 0.25),
        "grid_output": noise(streams_of[17], (C, C), C ** -0.5, 0.25),
        "grid_table": draw_grid_table(jax.random.fold_in(streams_of[22], 71), 0),
        "second_gain": jnp.clip(1.0 + 0.1 * jax.random.normal(streams_of[19], (C,), jnp.float32), 0.5, 1.5),
        "second_expand": noise(streams_of[20], (C, FF), C ** -0.5, 0.25),
        "second_reduce": noise(streams_of[21], (FF, C), FF ** -0.5, 0.125),
    }


def layer_norm_apply(values, norm_gain):
    widened = values.astype(jnp.float32)
    center = widened - lax.optimization_barrier(jnp.mean(widened, axis=-1, keepdims=True))
    spread = lax.optimization_barrier(jnp.mean(center * center, axis=-1, keepdims=True))
    return (center * lax.rsqrt(spread + 1e-05) * norm_gain).astype(jnp.bfloat16)

def position_bias(offset_bias_lookup):
    position = jnp.arange(WIN * WIN)
    down_pos = position // WIN
    across = position % WIN
    relative = (down_pos[:, None] - down_pos[None, :] + WIN - 1) * (2 * WIN - 1) + (across[:, None] - across[None, :] + WIN - 1)
    return offset_bias_lookup[:, relative]

def attend(triple, pos_bias):
    window_count, tokens, three_width = triple.shape
    feature_width = three_width // 3
    head_count = pos_bias.shape[0]
    head_size = feature_width // head_count
    queries = triple[..., :feature_width].reshape(window_count, tokens, head_count, head_size).astype(jnp.float32)
    key_row_list = triple[..., feature_width:2 * feature_width].reshape(window_count, tokens, head_count, head_size).astype(jnp.float32)
    values = triple[..., 2 * feature_width:].reshape(window_count, tokens, head_count, head_size).astype(jnp.float32)
    scores = jnp.einsum('nqhd,nkhd->nhqk', queries, key_row_list) * head_size ** (-0.5) + pos_bias[None]
    row_max = lax.optimization_barrier(jnp.max(scores, axis=-1, keepdims=True))
    weight_tensors = jnp.exp(scores - row_max)
    attention_weight_map = (weight_tensors / lax.optimization_barrier(jnp.sum(weight_tensors, axis=-1, keepdims=True))).astype(jnp.bfloat16)
    mixed = jnp.einsum('nhqk,nkhd->nqhd', attention_weight_map.astype(jnp.float32), values)
    return mixed.astype(jnp.bfloat16).reshape(window_count, tokens, feature_width)

def attention_sublayer(windows, norm_gain, in_weight, out_weight, pos_bias):
    normed = layer_norm_apply(windows, norm_gain)
    triple = jnp.dot(normed, in_weight, preferred_element_type=jnp.float32).astype(jnp.bfloat16)
    per_device = triple.shape[0] // (N_ROW * N_COL)
    grouped = triple.reshape(N_ROW * N_COL, per_device, WIN * WIN, triple.shape[-1])
    mixed = lax.map(lambda blocked: attend(blocked, pos_bias), grouped)
    mixed = mixed.reshape(windows.shape[0], WIN * WIN, -1)
    return (windows.astype(jnp.float32) + jnp.dot(mixed, out_weight, preferred_element_type=jnp.float32)).astype(jnp.bfloat16)

def feed_forward(values, norm_gain, in_weight, out_weight):
    normed = layer_norm_apply(values, norm_gain)
    hidden = jax.nn.gelu(jnp.dot(normed, in_weight, preferred_element_type=jnp.float32), approximate=True).astype(jnp.bfloat16)
    return (values.astype(jnp.float32) + jnp.dot(hidden, out_weight, preferred_element_type=jnp.float32)).astype(jnp.bfloat16)

def block_windows(field):
    feats = field.shape[-1]
    return field.reshape(HEIGHT // WIN, WIN, WIDTH // WIN, WIN, feats).transpose(0, 2, 1, 3, 4).reshape(-1, WIN * WIN, feats)

def block_field(windows):
    feats = windows.shape[-1]
    return windows.reshape(HEIGHT // WIN, WIDTH // WIN, WIN, WIN, feats).transpose(0, 2, 1, 3, 4).reshape(HEIGHT, WIDTH, feats)

def grid_windows(field):
    feats = field.shape[-1]
    return field.reshape(WIN, HEIGHT // WIN, WIN, WIDTH // WIN, feats).transpose(1, 3, 0, 2, 4).reshape(-1, WIN * WIN, feats)

def grid_field(windows):
    feats = windows.shape[-1]
    return windows.reshape(HEIGHT // WIN, WIDTH // WIN, WIN, WIN, feats).transpose(2, 0, 3, 1, 4).reshape(HEIGHT, WIDTH, feats)

def squeeze_gate(pooled, squeeze_down, squeeze_up):
    reduced = jax.nn.silu(jnp.dot(pooled[None, :], squeeze_down.astype(jnp.float32), precision=lax.Precision.HIGHEST))
    return jax.nn.sigmoid(jnp.dot(reduced, squeeze_up.astype(jnp.float32), precision=lax.Precision.HIGHEST))[0]

def reference(latent, conv_scale, conv_shift, expand_weight, depth_kernel, squeeze_down, squeeze_up, project_weight, block_gain, block_projection, block_output, block_table, first_gain, first_expand, first_reduce, grid_gain, grid_projection, grid_output, grid_table, second_gain, second_expand, second_reduce):
    conv_in = (latent.astype(jnp.float32) * conv_scale + conv_shift).astype(jnp.bfloat16)
    expanded = jax.nn.gelu(jnp.dot(conv_in, expand_weight, preferred_element_type=jnp.float32), approximate=True).astype(jnp.bfloat16)
    padded = jnp.pad(expanded, ((1, 1), (1, 1), (0, 0)))
    summed = jnp.zeros(expanded.shape, jnp.float32)
    for offset in range(9):
        down_step = offset // 3
        side_step = offset % 3
        summed = summed + padded[down_step:down_step + HEIGHT, side_step:side_step + WIDTH].astype(jnp.float32) * depth_kernel[offset]
    depthwise = jax.nn.gelu(summed, approximate=True)
    pooled = lax.optimization_barrier(jnp.sum(depthwise, axis=(0, 1))) / (HEIGHT * WIDTH)
    excite = squeeze_gate(pooled, squeeze_down, squeeze_up)
    gated = (depthwise * excite).astype(jnp.bfloat16)
    conv_out = (latent.astype(jnp.float32) + jnp.dot(gated, project_weight, preferred_element_type=jnp.float32)).astype(jnp.bfloat16)
    section = block_field(attention_sublayer(block_windows(conv_out), block_gain, block_projection, block_output, position_bias(block_table)))
    section = feed_forward(section, first_gain, first_expand, first_reduce)
    section = grid_field(attention_sublayer(grid_windows(section), grid_gain, grid_projection, grid_output, position_bias(grid_table)))
    return feed_forward(section, second_gain, second_expand, second_reduce)
```

```python
import functools

import jax
import jax.numpy as jnp
import numpy as np
from jax import lax
from jax.experimental import pallas as pl
from jax.experimental.pallas import tpu as pltpu
from jax.sharding import PartitionSpec as P

WIN = 8


def extended(cells, sides, width):
    for axis, dim in sides:
        count = lax.axis_size(axis)
        ends = count - 1
        head = lax.slice_in_dim(cells, 0, width, axis=dim)
        tail = lax.slice_in_dim(cells, cells.shape[dim] - width, cells.shape[dim], axis=dim)
        cells = jnp.concatenate(
            [
                lax.ppermute(tail, axis, [(i, (i + 1) % count) for i in range(ends)]),
                cells,
                lax.ppermute(head, axis, [((i + 1) % count, i) for i in range(ends)]),
            ],
            axis=dim,
        )
    return cells


def layer_norm_apply(values, norm_gain):
    widened = values.astype(jnp.float32)
    center = widened - jnp.mean(widened, axis=-1, keepdims=True)
    spread = jnp.mean(center * center, axis=-1, keepdims=True)
    return (center * lax.rsqrt(spread + 1e-05) * norm_gain).astype(jnp.bfloat16)


def position_bias(offset_bias_lookup):
    spots = offset_bias_lookup.shape[1]
    position = jnp.arange(WIN * WIN)
    down_pos = position // WIN
    across = position % WIN
    relative = (down_pos[:, None] - down_pos[None, :] + WIN - 1) * (2 * WIN - 1) + (
        across[:, None] - across[None, :] + WIN - 1
    )
    indicator_matrix = (relative[:, :, None] == jnp.arange(spots)[None, None, :]).astype(
        jnp.float32
    )
    return jnp.einsum(
        "bp,rjp->brj", offset_bias_lookup, indicator_matrix, precision=lax.Precision.HIGHEST
    )


def attend(triple, pos_bias):
    window_count, tokens, three_width = triple.shape
    feature_width = three_width // 3
    head_count = pos_bias.shape[0]
    head_size = feature_width // head_count
    queries = triple[..., :feature_width].reshape(window_count, tokens, head_count, head_size)
    key_row_list = triple[..., feature_width : 2 * feature_width].reshape(
        window_count, tokens, head_count, head_size
    )
    values = triple[..., 2 * feature_width :].reshape(window_count, tokens, head_count, head_size)
    scores = (
        jnp.einsum("nqhd,nkhd->nhqk", queries, key_row_list, preferred_element_type=jnp.float32)
        * head_size ** (-0.5)
        + pos_bias[None]
    )
    row_max = jnp.max(scores, axis=-1, keepdims=True)
    weight_tensors = jnp.exp(scores - row_max)
    attention_weight_map = (
        weight_tensors / jnp.sum(weight_tensors, axis=-1, keepdims=True)
    ).astype(jnp.bfloat16)
    mixed = jnp.einsum(
        "nhqk,nkhd->nqhd", attention_weight_map, values, preferred_element_type=jnp.float32
    )
    return mixed.astype(jnp.bfloat16).reshape(window_count, tokens, feature_width)


def attention_sublayer(windows, norm_gain, in_weight, out_weight, pos_bias):
    normed = layer_norm_apply(windows, norm_gain)
    triple = jnp.dot(normed, in_weight, preferred_element_type=jnp.float32).astype(jnp.bfloat16)
    mixed = attend(triple, pos_bias)
    return (
        windows.astype(jnp.float32) + jnp.dot(mixed, out_weight, preferred_element_type=jnp.float32)
    ).astype(jnp.bfloat16)


def feed_forward(values, norm_gain, in_weight, out_weight):
    normed = layer_norm_apply(values, norm_gain)
    hidden = jax.nn.gelu(
        jnp.dot(normed, in_weight, preferred_element_type=jnp.float32), approximate=True
    ).astype(jnp.bfloat16)
    return (
        values.astype(jnp.float32) + jnp.dot(hidden, out_weight, preferred_element_type=jnp.float32)
    ).astype(jnp.bfloat16)


def to_blocks(field):
    row_count, col_count, feats = field.shape
    return (
        field.reshape(row_count // WIN, WIN, col_count // WIN, WIN, feats)
        .transpose(0, 2, 1, 3, 4)
        .reshape(-1, WIN * WIN, feats)
    )


def from_blocks(windows, row_count, col_count):
    feats = windows.shape[-1]
    return (
        windows.reshape(row_count // WIN, col_count // WIN, WIN, WIN, feats)
        .transpose(0, 2, 1, 3, 4)
        .reshape(row_count, col_count, feats)
    )


def axis_shape(length, devices):
    fold = max(1, WIN // devices)
    rest = length // max(devices, WIN)
    span = min(devices, WIN)
    return (fold, rest, span, devices // span)


def grid_layout(field):
    row_devices = lax.axis_size("row")
    col_devices = lax.axis_size("col")
    row_count, col_count, feats = field.shape
    row_fold, row_rest, row_span, row_hop = axis_shape(row_count, row_devices)
    col_fold, col_rest, col_span, col_hop = axis_shape(col_count, col_devices)
    ordered_layout = field.reshape(
        row_fold, row_devices, row_rest, col_fold, col_devices, col_rest, feats
    )
    flat = ordered_layout.transpose(1, 4, 0, 2, 3, 5, 6).reshape(
        row_devices * col_devices, row_fold, row_rest, col_fold, col_rest, feats
    )
    flat = lax.all_to_all(flat, ("row", "col"), split_axis=0, concat_axis=0, tiled=True)
    moved = flat.reshape(
        row_devices, col_devices, row_fold, row_rest, col_fold, col_rest, feats
    ).transpose(2, 0, 3, 4, 1, 5, 6)
    moved = moved.reshape(
        row_fold, row_span, row_hop, row_rest, col_fold, col_span, col_hop, col_rest, feats
    )
    return moved.transpose(2, 3, 6, 7, 1, 0, 5, 4, 8).reshape(-1, WIN * WIN, feats)


def spatial_layout(windows, row_count, col_count):
    row_devices = lax.axis_size("row")
    col_devices = lax.axis_size("col")
    feats = windows.shape[-1]
    row_fold, row_rest, row_span, row_hop = axis_shape(row_count, row_devices)
    col_fold, col_rest, col_span, col_hop = axis_shape(col_count, col_devices)
    gridded = windows.reshape(
        row_hop, row_rest, col_hop, col_rest, row_span, row_fold, col_span, col_fold, feats
    )
    ordered_layout = gridded.transpose(5, 4, 0, 1, 7, 6, 2, 3, 8).reshape(
        row_fold, row_devices, row_rest, col_fold, col_devices, col_rest, feats
    )
    flat = ordered_layout.transpose(1, 4, 0, 2, 3, 5, 6).reshape(
        row_devices * col_devices, row_fold, row_rest, col_fold, col_rest, feats
    )
    flat = lax.all_to_all(flat, ("row", "col"), split_axis=0, concat_axis=0, tiled=True)
    moved = flat.reshape(
        row_devices, col_devices, row_fold, row_rest, col_fold, col_rest, feats
    ).transpose(2, 0, 3, 4, 1, 5, 6)
    return moved.reshape(row_count, col_count, feats)


def squeeze_gate(pooled, squeeze_down, squeeze_up):
    reduced = jax.nn.silu(
        jnp.dot(pooled[None, :], squeeze_down.astype(jnp.float32), precision=lax.Precision.HIGHEST)
    )
    return jax.nn.sigmoid(
        jnp.dot(reduced, squeeze_up.astype(jnp.float32), precision=lax.Precision.HIGHEST)
    )[0]


def axis_sum_kernel(axis, count, x_ref, o_ref, slots, send_sem, recv_sem):
    me = lax.axis_index(axis)
    barrier = pltpu.get_barrier_semaphore()
    peers = [lax.rem(me + step, count) for step in range(1, count)]
    for peer in peers:
        pl.semaphore_signal(
            barrier, inc=1, device_id={axis: peer}, device_id_type=pl.DeviceIdType.MESH
        )
    pl.semaphore_wait(barrier, count - 1)
    copies = []
    for step, peer in enumerate(peers):
        copy = pltpu.make_async_remote_copy(
            src_ref=x_ref,
            dst_ref=slots.at[step],
            send_sem=send_sem.at[step],
            recv_sem=recv_sem.at[step],
            device_id={axis: peer},
            device_id_type=pl.DeviceIdType.MESH,
        )
        copy.start()
        copies.append(copy)
    for copy in copies:
        copy.wait()
    total = x_ref[...]
    for step in range(count - 1):
        total = total + slots[step]
    o_ref[...] = total


def axis_sum(values, axis, collective_id):
    count = lax.axis_size(axis)
    if count == 1:
        return values
    return pl.pallas_call(
        functools.partial(axis_sum_kernel, axis, count),
        out_shape=jax.ShapeDtypeStruct(values.shape, values.dtype),
        in_specs=[pl.BlockSpec(memory_space=pltpu.VMEM)],
        out_specs=pl.BlockSpec(memory_space=pltpu.VMEM),
        scratch_shapes=[
            pltpu.VMEM((count - 1,) + values.shape, values.dtype),
            pltpu.SemaphoreType.DMA((count - 1,)),
            pltpu.SemaphoreType.DMA((count - 1,)),
        ],
        compiler_params=pltpu.CompilerParams(collective_id=collective_id, has_side_effects=True),
        name="axis_sum_" + axis,
    )(values)


LANES = 128
GROUP = 256


def normed_rows(widened, gain):
    center = widened - jnp.mean(widened, axis=-1, keepdims=True)
    spread = jnp.mean(center * center, axis=-1, keepdims=True)
    return (center * lax.rsqrt(spread + 1e-05) * gain).astype(jnp.bfloat16)


def mixer_kernel(
    layout, head_size, x_ref, gain_ref, bias_ref, late_gain_ref, proj_hbm, out_hbm, up_hbm, down_hbm,
    o_ref, triple, heads, proj_ref, out_w_ref, up_ref, down_ref, sems,
):
    kind, across = layout
    rows_total, feats = x_ref.shape
    tokens = WIN * WIN
    window_count = rows_total // tokens
    slabs = feats // LANES
    per_slab = LANES // head_size
    moves = [
        pltpu.make_async_copy(src, dst, sems.at[k])
        for k, (src, dst) in enumerate(
            ((proj_hbm, proj_ref), (out_hbm, out_w_ref), (up_hbm, up_ref), (down_hbm, down_ref))
        )
    ]
    for move in moves:
        move.start()
    moves[0].wait()
    chunk = 256

    def project(step, carry):
        rows = pl.ds(pl.multiple_of(step * chunk, chunk), chunk)
        normed = normed_rows(x_ref[rows, :].astype(jnp.float32), gain_ref[...])
        for part in range(3 * slabs // 2):
            product = jnp.dot(
                normed, proj_ref[:, part * GROUP : (part + 1) * GROUP],
                preferred_element_type=jnp.float32,
            ).astype(jnp.bfloat16).astype(jnp.float32)
            triple[2 * part, rows, :] = product[:, :LANES]
            triple[2 * part + 1, rows, :] = product[:, LANES:]
        return carry

    lax.fori_loop(0, rows_total // chunk, project, 0)

    def places(window):
        if kind == "strided":
            return [pl.ds(window, tokens, stride=across)]
        per_row = across // WIN
        base = (window // per_row) * (WIN * across) + (window % per_row) * WIN
        return [pl.ds(pl.multiple_of(base + r * across, WIN), WIN) for r in range(WIN)]

    lane = lax.broadcasted_iota(jnp.int32, (tokens, GROUP), 1)
    head_of = (lane % LANES) // head_size
    scale = head_size ** (-0.5)

    def one_window(window):
        spots = places(window)

        def fetch(slab):
            pieces = [triple[slab, spot, :] for spot in spots]
            whole = pieces[0] if len(pieces) == 1 else jnp.concatenate(pieces, axis=0)
            return whole

        empty = jnp.zeros((tokens, LANES), jnp.bfloat16)
        for group in range(slabs // 2):
            first, second = 2 * group, 2 * group + 1
            query_0 = fetch(first).astype(jnp.bfloat16)
            query_1 = fetch(second).astype(jnp.bfloat16)
            keys = jnp.concatenate([fetch(slabs + first), fetch(slabs + second)], axis=1)
            vals = jnp.concatenate([fetch(2 * slabs + first), fetch(2 * slabs + second)], axis=1)
            block_q = jnp.concatenate(
                [
                    jnp.concatenate([query_0, empty], axis=1),
                    jnp.concatenate([empty, query_1], axis=1),
                ],
                axis=0,
            )
            block_k = jnp.concatenate(
                [jnp.where(head_of == j, keys, 0.0).astype(jnp.bfloat16) for j in range(per_slab)],
                axis=0,
            )
            block_v = jnp.concatenate(
                [jnp.where(head_of == j, vals, 0.0).astype(jnp.bfloat16) for j in range(per_slab)],
                axis=0,
            )
            scores = lax.dot_general(
                block_k, block_q, (((1,), (1,)), ((), ())), preferred_element_type=jnp.float32
            )
            scores = (scores * scale + bias_ref[group]).reshape(per_slab, tokens, 2 * tokens)
            weights = jnp.exp(scores - jnp.max(scores, axis=1, keepdims=True))
            shares = weights / jnp.sum(weights, axis=1, keepdims=True)
            shares = shares.reshape(per_slab * tokens, 2 * tokens).astype(jnp.bfloat16)
            mixed = lax.dot_general(
                shares, block_v, (((0,), (0,)), ((), ())), preferred_element_type=jnp.float32
            )
            for slab, part in (
                (first, mixed[:tokens, :LANES]), (second, mixed[tokens:, LANES:])
            ):
                if len(spots) == 1:
                    heads[slab, spots[0], :] = part
                else:
                    for r, spot in enumerate(spots):
                        heads[slab, spot, :] = part[r * WIN : (r + 1) * WIN]

    def attend_pair(step, carry):
        one_window(2 * step)
        one_window(2 * step + 1)
        return carry

    lax.fori_loop(0, window_count // 2, attend_pair, 0)
    for move in moves[1:]:
        move.wait()
    hidden_width = up_ref.shape[1]
    tile = 512

    def feed(step, carry):
        rows = pl.ds(pl.multiple_of(step * chunk, chunk), chunk)
        mixed = jnp.concatenate([heads[s, rows, :] for s in range(slabs)], axis=1).astype(jnp.bfloat16)
        value = (
            x_ref[rows, :].astype(jnp.float32)
            + jnp.dot(mixed, out_w_ref[...], preferred_element_type=jnp.float32)
        ).astype(jnp.bfloat16).astype(jnp.float32)
        normed = normed_rows(value, late_gain_ref[...])
        for k in range(hidden_width // tile):
            part = slice(k * tile, (k + 1) * tile)
            hidden = jax.nn.gelu(
                jnp.dot(normed, up_ref[:, part], preferred_element_type=jnp.float32),
                approximate=True,
            ).astype(jnp.bfloat16)
            value = value + jnp.dot(hidden, down_ref[part, :], preferred_element_type=jnp.float32)
        o_ref[rows, :] = value.astype(jnp.bfloat16)
        return carry

    lax.fori_loop(0, rows_total // chunk, feed, 0)


def mixer(x, layout, gain, in_weight, out_weight, bias, late_gain, up, down, heads_count):
    rows, feats = x.shape
    vmem = pl.BlockSpec(memory_space=pltpu.VMEM)
    hbm = pl.BlockSpec(memory_space=pl.ANY)
    flops = 2 * rows * feats * (4 * feats + 2 * up.shape[1])
    return pl.pallas_call(
        functools.partial(mixer_kernel, layout, feats // heads_count),
        out_shape=jax.ShapeDtypeStruct((rows, feats), jnp.bfloat16),
        in_specs=[vmem] * 4 + [hbm] * 4,
        out_specs=vmem,
        scratch_shapes=[
            pltpu.VMEM((3 * feats // LANES, rows, LANES), jnp.float32),
            pltpu.VMEM((feats // LANES, rows, LANES), jnp.float32),
            pltpu.VMEM(in_weight.shape, jnp.bfloat16),
            pltpu.VMEM(out_weight.shape, jnp.bfloat16),
            pltpu.VMEM(up.shape, jnp.bfloat16),
            pltpu.VMEM(down.shape, jnp.bfloat16),
            pltpu.SemaphoreType.DMA((4,)),
        ],
        compiler_params=pltpu.CompilerParams(vmem_limit_bytes=48 * 1024 * 1024),
        cost_estimate=pl.CostEstimate(
            flops=flops, bytes_accessed=12 * 1024 * 1024, transcendentals=0
        ),
        name="mixer_" + layout[0],
    )(x, gain[None], bias, late_gain[None], in_weight, out_weight, up, down)


def key_major_bias(table, down, across):
    head_count, spots = table.shape
    relative = (down[None, :] - down[:, None] + WIN - 1) * (2 * WIN - 1) + (
        across[None, :] - across[:, None] + WIN - 1
    )
    tokens = WIN * WIN
    chosen = (jnp.arange(spots)[:, None] == jnp.asarray(relative.reshape(-1))[None, :]).astype(
        jnp.float32
    )
    spread = jnp.dot(table, chosen, precision=lax.Precision.HIGHEST)
    return (
        spread.reshape(head_count // 8, 2, 4, tokens, tokens)
        .transpose(0, 2, 3, 1, 4)
        .reshape(head_count // 8, 4 * tokens, 2 * tokens)
    )


def grid_sublayers(section, run, grid_table):
    row_devices = lax.axis_size("row")
    col_devices = lax.axis_size("col")
    row_count, col_count, feats = section.shape
    plain = np.arange(WIN * WIN)
    if row_devices > WIN or col_devices > WIN:
        windows = grid_layout(section)
        count = windows.shape[0]
        bias = key_major_bias(grid_table, plain // WIN, plain % WIN)
        out = run(windows.transpose(1, 0, 2).reshape(-1, feats), ("strided", count), bias)
        out = out.reshape(WIN * WIN, count, feats).transpose(1, 0, 2)
        return spatial_layout(out, row_count, col_count)
    devices = row_devices * col_devices
    row_fold, col_fold = WIN // row_devices, WIN // col_devices
    row_rest, col_rest = row_count // row_fold, col_count // col_fold
    count = row_rest * col_rest // devices
    pieces = col_rest // count
    sent = (
        section.reshape(row_fold, row_rest, col_fold, pieces, count, feats)
        .transpose(1, 3, 0, 2, 4, 5)
        .reshape(devices, row_fold * col_fold * count, feats)
    )
    got = lax.all_to_all(sent, ("row", "col"), split_axis=0, concat_axis=0, tiled=True)
    order = np.arange(WIN * WIN).reshape(row_devices, col_devices, row_fold, col_fold)
    at = np.indices(order.shape).reshape(4, -1)
    bias = key_major_bias(grid_table, at[0] * row_fold + at[2], at[1] * col_fold + at[3])
    out = run(got.reshape(-1, feats), ("strided", count), bias)
    back = lax.all_to_all(
        out.reshape(devices, -1, feats), ("row", "col"), split_axis=0, concat_axis=0, tiled=True
    )
    return (
        back.reshape(row_rest, pieces, row_fold, col_fold, count, feats)
        .transpose(2, 0, 3, 1, 4, 5)
        .reshape(row_count, col_count, feats)
    )


def per_device(
    latent,
    conv_scale,
    conv_shift,
    expand_weight,
    depth_kernel,
    squeeze_down,
    squeeze_up,
    project_weight,
    block_gain,
    block_projection,
    block_output,
    block_table,
    first_gain,
    first_expand,
    first_reduce,
    grid_gain,
    grid_projection,
    grid_output,
    grid_table,
    second_gain,
    second_expand,
    second_reduce,
):
    row_devices = lax.axis_size("row")
    col_devices = lax.axis_size("col")
    row_count, col_count, channels = latent.shape
    conv_in = (latent.astype(jnp.float32) * conv_scale + conv_shift).astype(jnp.bfloat16)
    expanded = jax.nn.gelu(
        jnp.dot(conv_in, expand_weight, preferred_element_type=jnp.float32), approximate=True
    ).astype(jnp.bfloat16)
    padded = extended(expanded, (("row", 0), ("col", 1)), 1)
    summed = jnp.zeros((row_count, col_count, padded.shape[-1]), jnp.float32)
    for offset in range(9):
        down_step = offset // 3
        side_step = offset % 3
        summed = (
            summed
            + padded[down_step : down_step + row_count, side_step : side_step + col_count].astype(
                jnp.float32
            )
            * depth_kernel[offset]
        )
    depthwise = jax.nn.gelu(summed, approximate=True)
    local_sums = jnp.sum(depthwise, axis=(0, 1)).reshape(-1, 128)
    channel_sums = axis_sum(axis_sum(local_sums, "row", 1), "col", 2).reshape(-1)
    pooled = channel_sums / (row_count * row_devices * col_count * col_devices)
    excite = squeeze_gate(pooled, squeeze_down, squeeze_up)
    gated = (depthwise * excite).astype(jnp.bfloat16)
    conv_out = (
        latent.astype(jnp.float32)
        + jnp.dot(gated, project_weight, preferred_element_type=jnp.float32)
    ).astype(jnp.bfloat16)
    plain = np.arange(WIN * WIN)
    section = mixer(
        conv_out.reshape(-1, channels), ("blocks", col_count), block_gain, block_projection,
        block_output, key_major_bias(block_table, plain // WIN, plain % WIN), first_gain,
        first_expand, first_reduce, block_table.shape[0],
    ).reshape(row_count, col_count, channels)

    def run(cells, layout, bias):
        return mixer(
            cells, layout, grid_gain, grid_projection, grid_output, bias, second_gain,
            second_expand, second_reduce, grid_table.shape[0],
        )

    return grid_sublayers(section, run, grid_table)


def solution(mesh):
    placed = (
        P("row", "col", None),
        P(),
        P(),
        P(),
        P(),
        P(),
        P(),
        P(),
        P(),
        P(),
        P(),
        P(),
        P(),
        P(),
        P(),
        P(),
        P(),
        P(),
        P(),
        P(),
        P(),
        P(),
    )
    return jax.shard_map(
        per_device, mesh=mesh, in_specs=placed, out_specs=P("row", "col", None), check_vma=False
    )
```

```python
import functools

import jax
import jax.numpy as jnp
import numpy as np
from jax import lax
from jax.experimental import pallas as pl
from jax.experimental.pallas import tpu as pltpu
from jax.sharding import PartitionSpec as P

WIN = 8


def extended(cells, sides, width):
    for axis, dim in sides:
        count = lax.axis_size(axis)
        ends = count - 1
        head = lax.slice_in_dim(cells, 0, width, axis=dim)
        tail = lax.slice_in_dim(cells, cells.shape[dim] - width, cells.shape[dim], axis=dim)
        cells = jnp.concatenate(
            [
                lax.ppermute(tail, axis, [(i, (i + 1) % count) for i in range(ends)]),
                cells,
                lax.ppermute(head, axis, [((i + 1) % count, i) for i in range(ends)]),
            ],
            axis=dim,
        )
    return cells


def layer_norm_apply(values, norm_gain):
    widened = values.astype(jnp.float32)
    center = widened - jnp.mean(widened, axis=-1, keepdims=True)
    spread = jnp.mean(center * center, axis=-1, keepdims=True)
    return (center * lax.rsqrt(spread + 1e-05) * norm_gain).astype(jnp.bfloat16)


def position_bias(offset_bias_lookup):
    spots = offset_bias_lookup.shape[1]
    position = jnp.arange(WIN * WIN)
    down_pos = position // WIN
    across = position % WIN
    relative = (down_pos[:, None] - down_pos[None, :] + WIN - 1) * (2 * WIN - 1) + (
        across[:, None] - across[None, :] + WIN - 1
    )
    indicator_matrix = (relative[:, :, None] == jnp.arange(spots)[None, None, :]).astype(
        jnp.float32
    )
    return jnp.einsum(
        "bp,rjp->brj", offset_bias_lookup, indicator_matrix, precision=lax.Precision.HIGHEST
    )


def attend(triple, pos_bias):
    window_count, tokens, three_width = triple.shape
    feature_width = three_width // 3
    head_count = pos_bias.shape[0]
    head_size = feature_width // head_count
    queries = triple[..., :feature_width].reshape(window_count, tokens, head_count, head_size)
    key_row_list = triple[..., feature_width : 2 * feature_width].reshape(
        window_count, tokens, head_count, head_size
    )
    values = triple[..., 2 * feature_width :].reshape(window_count, tokens, head_count, head_size)
    scores = (
        jnp.einsum("nqhd,nkhd->nhqk", queries, key_row_list, preferred_element_type=jnp.float32)
        * head_size ** (-0.5)
        + pos_bias[None]
    )
    row_max = jnp.max(scores, axis=-1, keepdims=True)
    weight_tensors = jnp.exp(scores - row_max)
    attention_weight_map = (
        weight_tensors / jnp.sum(weight_tensors, axis=-1, keepdims=True)
    ).astype(jnp.bfloat16)
    mixed = jnp.einsum(
        "nhqk,nkhd->nqhd", attention_weight_map, values, preferred_element_type=jnp.float32
    )
    return mixed.astype(jnp.bfloat16).reshape(window_count, tokens, feature_width)


def attention_sublayer(windows, norm_gain, in_weight, out_weight, pos_bias):
    normed = layer_norm_apply(windows, norm_gain)
    triple = jnp.dot(normed, in_weight, preferred_element_type=jnp.float32).astype(jnp.bfloat16)
    mixed = attend(triple, pos_bias)
    return (
        windows.astype(jnp.float32) + jnp.dot(mixed, out_weight, preferred_element_type=jnp.float32)
    ).astype(jnp.bfloat16)


def feed_forward(values, norm_gain, in_weight, out_weight):
    normed = layer_norm_apply(values, norm_gain)
    hidden = jax.nn.gelu(
        jnp.dot(normed, in_weight, preferred_element_type=jnp.float32), approximate=True
    ).astype(jnp.bfloat16)
    return (
        values.astype(jnp.float32) + jnp.dot(hidden, out_weight, preferred_element_type=jnp.float32)
    ).astype(jnp.bfloat16)


def to_blocks(field):
    row_count, col_count, feats = field.shape
    return (
        field.reshape(row_count // WIN, WIN, col_count // WIN, WIN, feats)
        .transpose(0, 2, 1, 3, 4)
        .reshape(-1, WIN * WIN, feats)
    )


def from_blocks(windows, row_count, col_count):
    feats = windows.shape[-1]
    return (
        windows.reshape(row_count // WIN, col_count // WIN, WIN, WIN, feats)
        .transpose(0, 2, 1, 3, 4)
        .reshape(row_count, col_count, feats)
    )


def axis_shape(length, devices):
    fold = max(1, WIN // devices)
    rest = length // max(devices, WIN)
    span = min(devices, WIN)
    return (fold, rest, span, devices // span)


def grid_layout(field):
    row_devices = lax.axis_size("row")
    col_devices = lax.axis_size("col")
    row_count, col_count, feats = field.shape
    row_fold, row_rest, row_span, row_hop = axis_shape(row_count, row_devices)
    col_fold, col_rest, col_span, col_hop = axis_shape(col_count, col_devices)
    ordered_layout = field.reshape(
        row_fold, row_devices, row_rest, col_fold, col_devices, col_rest, feats
    )
    flat = ordered_layout.transpose(1, 4, 0, 2, 3, 5, 6).reshape(
        row_devices * col_devices, row_fold, row_rest, col_fold, col_rest, feats
    )
    flat = lax.all_to_all(flat, ("row", "col"), split_axis=0, concat_axis=0, tiled=True)
    moved = flat.reshape(
        row_devices, col_devices, row_fold, row_rest, col_fold, col_rest, feats
    ).transpose(2, 0, 3, 4, 1, 5, 6)
    moved = moved.reshape(
        row_fold, row_span, row_hop, row_rest, col_fold, col_span, col_hop, col_rest, feats
    )
    return moved.transpose(2, 3, 6, 7, 1, 0, 5, 4, 8).reshape(-1, WIN * WIN, feats)


def spatial_layout(windows, row_count, col_count):
    row_devices = lax.axis_size("row")
    col_devices = lax.axis_size("col")
    feats = windows.shape[-1]
    row_fold, row_rest, row_span, row_hop = axis_shape(row_count, row_devices)
    col_fold, col_rest, col_span, col_hop = axis_shape(col_count, col_devices)
    gridded = windows.reshape(
        row_hop, row_rest, col_hop, col_rest, row_span, row_fold, col_span, col_fold, feats
    )
    ordered_layout = gridded.transpose(5, 4, 0, 1, 7, 6, 2, 3, 8).reshape(
        row_fold, row_devices, row_rest, col_fold, col_devices, col_rest, feats
    )
    flat = ordered_layout.transpose(1, 4, 0, 2, 3, 5, 6).reshape(
        row_devices * col_devices, row_fold, row_rest, col_fold, col_rest, feats
    )
    flat = lax.all_to_all(flat, ("row", "col"), split_axis=0, concat_axis=0, tiled=True)
    moved = flat.reshape(
        row_devices, col_devices, row_fold, row_rest, col_fold, col_rest, feats
    ).transpose(2, 0, 3, 4, 1, 5, 6)
    return moved.reshape(row_count, col_count, feats)


def squeeze_gate(pooled, squeeze_down, squeeze_up):
    reduced = jax.nn.silu(
        jnp.dot(pooled[None, :], squeeze_down.astype(jnp.float32), precision=lax.Precision.HIGHEST)
    )
    return jax.nn.sigmoid(
        jnp.dot(reduced, squeeze_up.astype(jnp.float32), precision=lax.Precision.HIGHEST)
    )[0]


def axis_sum_kernel(axis, count, x_ref, o_ref, slots, send_sem, recv_sem):
    me = lax.axis_index(axis)
    barrier = pltpu.get_barrier_semaphore()
    peers = [lax.rem(me + step, count) for step in range(1, count)]
    for peer in peers:
        pl.semaphore_signal(
            barrier, inc=1, device_id={axis: peer}, device_id_type=pl.DeviceIdType.MESH
        )
    pl.semaphore_wait(barrier, count - 1)
    copies = []
    for step, peer in enumerate(peers):
        copy = pltpu.make_async_remote_copy(
            src_ref=x_ref,
            dst_ref=slots.at[step],
            send_sem=send_sem.at[step],
            recv_sem=recv_sem.at[step],
            device_id={axis: peer},
            device_id_type=pl.DeviceIdType.MESH,
        )
        copy.start()
        copies.append(copy)
    for copy in copies:
        copy.wait()
    total = x_ref[...]
    for step in range(count - 1):
        total = total + slots[step]
    o_ref[...] = total


def axis_sum(values, axis, collective_id):
    count = lax.axis_size(axis)
    if count == 1:
        return values
    return pl.pallas_call(
        functools.partial(axis_sum_kernel, axis, count),
        out_shape=jax.ShapeDtypeStruct(values.shape, values.dtype),
        in_specs=[pl.BlockSpec(memory_space=pltpu.VMEM)],
        out_specs=pl.BlockSpec(memory_space=pltpu.VMEM),
        scratch_shapes=[
            pltpu.VMEM((count - 1,) + values.shape, values.dtype),
            pltpu.SemaphoreType.DMA((count - 1,)),
            pltpu.SemaphoreType.DMA((count - 1,)),
        ],
        compiler_params=pltpu.CompilerParams(collective_id=collective_id, has_side_effects=True),
        name="axis_sum_" + axis,
    )(values)


LANES = 128
GROUP = 256


def normed_rows(widened, gain):
    center = widened - jnp.mean(widened, axis=-1, keepdims=True)
    spread = jnp.mean(center * center, axis=-1, keepdims=True)
    return (center * lax.rsqrt(spread + 1e-05) * gain).astype(jnp.bfloat16)


def mixer_kernel(
    layout, head_size, x_ref, gain_ref, bias_ref, late_gain_ref, proj_hbm, out_hbm, up_hbm, down_hbm,
    o_ref, triple, heads, proj_ref, out_w_ref, up_ref, down_ref, sems,
):
    kind, across = layout
    rows_total, feats = x_ref.shape
    tokens = WIN * WIN
    window_count = rows_total // tokens
    slabs = feats // LANES
    per_slab = LANES // head_size
    moves = [
        pltpu.make_async_copy(src, dst, sems.at[k])
        for k, (src, dst) in enumerate(
            ((proj_hbm, proj_ref), (out_hbm, out_w_ref), (up_hbm, up_ref), (down_hbm, down_ref))
        )
    ]
    for move in moves:
        move.start()
    moves[0].wait()
    chunk = 256

    def project(step, carry):
        rows = pl.ds(pl.multiple_of(step * chunk, chunk), chunk)
        normed = normed_rows(x_ref[rows, :].astype(jnp.float32), gain_ref[...])
        for part in range(3 * slabs // 2):
            product = jnp.dot(
                normed, proj_ref[:, part * GROUP : (part + 1) * GROUP],
                preferred_element_type=jnp.float32,
            ).astype(jnp.bfloat16).astype(jnp.float32)
            triple[2 * part, rows, :] = product[:, :LANES]
            triple[2 * part + 1, rows, :] = product[:, LANES:]
        return carry

    lax.fori_loop(0, rows_total // chunk, project, 0)

    def places(window):
        if kind == "strided":
            return [pl.ds(window, tokens, stride=across)]
        per_row = across // WIN
        base = (window // per_row) * (WIN * across) + (window % per_row) * WIN
        return [pl.ds(pl.multiple_of(base + r * across, WIN), WIN) for r in range(WIN)]

    lane = lax.broadcasted_iota(jnp.int32, (tokens, GROUP), 1)
    head_of = (lane % LANES) // head_size
    scale = head_size ** (-0.5)

    def one_window(window):
        spots = places(window)

        def fetch(slab):
            pieces = [triple[slab, spot, :] for spot in spots]
            whole = pieces[0] if len(pieces) == 1 else jnp.concatenate(pieces, axis=0)
            return whole

        empty = jnp.zeros((tokens, LANES), jnp.bfloat16)
        for group in range(slabs // 2):
            first, second = 2 * group, 2 * group + 1
            query_0 = fetch(first).astype(jnp.bfloat16)
            query_1 = fetch(second).astype(jnp.bfloat16)
            keys = jnp.concatenate([fetch(slabs + first), fetch(slabs + second)], axis=1)
            vals = jnp.concatenate([fetch(2 * slabs + first), fetch(2 * slabs + second)], axis=1)
            block_q = jnp.concatenate(
                [
                    jnp.concatenate([query_0, empty], axis=1),
                    jnp.concatenate([empty, query_1], axis=1),
                ],
                axis=0,
            )
            block_k = jnp.concatenate(
                [jnp.where(head_of == j, keys, 0.0).astype(jnp.bfloat16) for j in range(per_slab)],
                axis=0,
            )
            block_v = jnp.concatenate(
                [jnp.where(head_of == j, vals, 0.0).astype(jnp.bfloat16) for j in range(per_slab)],
                axis=0,
            )
            scores = lax.dot_general(
                block_k, block_q, (((1,), (1,)), ((), ())), preferred_element_type=jnp.float32
            )
            scores = (scores * scale + bias_ref[group]).reshape(per_slab, tokens, 2 * tokens)
            weights = jnp.exp(scores - jnp.max(scores, axis=1, keepdims=True))
            shares = weights / jnp.sum(weights, axis=1, keepdims=True)
            shares = shares.reshape(per_slab * tokens, 2 * tokens).astype(jnp.bfloat16)
            mixed = lax.dot_general(
                shares, block_v, (((0,), (0,)), ((), ())), preferred_element_type=jnp.float32
            )
            for slab, part in (
                (first, mixed[:tokens, :LANES]), (second, mixed[tokens:, LANES:])
            ):
                if len(spots) == 1:
                    heads[slab, spots[0], :] = part
                else:
                    for r, spot in enumerate(spots):
                        heads[slab, spot, :] = part[r * WIN : (r + 1) * WIN]

    def attend_pair(step, carry):
        one_window(2 * step)
        one_window(2 * step + 1)
        return carry

    lax.fori_loop(0, window_count // 2, attend_pair, 0)
    for move in moves[1:]:
        move.wait()
    hidden_width = up_ref.shape[1]
    tile = 512

    def feed(step, carry):
        rows = pl.ds(pl.multiple_of(step * chunk, chunk), chunk)
        mixed = jnp.concatenate([heads[s, rows, :] for s in range(slabs)], axis=1).astype(jnp.bfloat16)
        value = (
            x_ref[rows, :].astype(jnp.float32)
            + jnp.dot(mixed, out_w_ref[...], preferred_element_type=jnp.float32)
        ).astype(jnp.bfloat16).astype(jnp.float32)
        normed = normed_rows(value, late_gain_ref[...])
        for k in range(hidden_width // tile):
            part = slice(k * tile, (k + 1) * tile)
            hidden = jax.nn.gelu(
                jnp.dot(normed, up_ref[:, part], preferred_element_type=jnp.float32),
                approximate=True,
            ).astype(jnp.bfloat16)
            value = value + jnp.dot(hidden, down_ref[part, :], preferred_element_type=jnp.float32)
        o_ref[rows, :] = value.astype(jnp.bfloat16)
        return carry

    lax.fori_loop(0, rows_total // chunk, feed, 0)


def mixer(x, layout, gain, in_weight, out_weight, bias, late_gain, up, down, heads_count):
    rows, feats = x.shape
    vmem = pl.BlockSpec(memory_space=pltpu.VMEM)
    hbm = pl.BlockSpec(memory_space=pl.ANY)
    flops = 8 * rows * feats * (4 * feats + 2 * up.shape[1])
    return pl.pallas_call(
        functools.partial(mixer_kernel, layout, feats // heads_count),
        out_shape=jax.ShapeDtypeStruct((rows, feats), jnp.bfloat16),
        in_specs=[vmem] * 4 + [hbm] * 4,
        out_specs=vmem,
        scratch_shapes=[
            pltpu.VMEM((3 * feats // LANES, rows, LANES), jnp.float32),
            pltpu.VMEM((feats // LANES, rows, LANES), jnp.float32),
            pltpu.VMEM(in_weight.shape, jnp.bfloat16),
            pltpu.VMEM(out_weight.shape, jnp.bfloat16),
            pltpu.VMEM(up.shape, jnp.bfloat16),
            pltpu.VMEM(down.shape, jnp.bfloat16),
            pltpu.SemaphoreType.DMA((4,)),
        ],
        compiler_params=pltpu.CompilerParams(vmem_limit_bytes=48 * 1024 * 1024),
        cost_estimate=pl.CostEstimate(
            flops=flops, bytes_accessed=12 * 1024 * 1024, transcendentals=0
        ),
        name="mixer_" + layout[0],
    )(x, gain[None], bias, late_gain[None], in_weight, out_weight, up, down)


def key_major_bias(table, down, across):
    head_count, spots = table.shape
    relative = (down[None, :] - down[:, None] + WIN - 1) * (2 * WIN - 1) + (
        across[None, :] - across[:, None] + WIN - 1
    )
    tokens = WIN * WIN
    chosen = (jnp.arange(spots)[:, None] == jnp.asarray(relative.reshape(-1))[None, :]).astype(
        jnp.float32
    )
    spread = jnp.dot(table, chosen, precision=lax.Precision.HIGHEST)
    return (
        spread.reshape(head_count // 8, 2, 4, tokens, tokens)
        .transpose(0, 2, 3, 1, 4)
        .reshape(head_count // 8, 4 * tokens, 2 * tokens)
    )


def split_sublayers(conv_out, run_block, run_grid, block_table, grid_table):
    row_devices = lax.axis_size("row")
    col_devices = lax.axis_size("col")
    row_count, col_count, feats = conv_out.shape
    plain = np.arange(WIN * WIN)
    block_bias = key_major_bias(block_table, plain // WIN, plain % WIN)
    if row_devices > WIN or col_devices > WIN:
        section = run_block(conv_out.reshape(-1, feats), ("blocks", col_count), block_bias)
        windows = grid_layout(section.reshape(row_count, col_count, feats))
        count = windows.shape[0]
        bias = key_major_bias(grid_table, plain // WIN, plain % WIN)
        out = run_grid(windows.transpose(1, 0, 2).reshape(-1, feats), ("strided", count), bias)
        out = out.reshape(WIN * WIN, count, feats).transpose(1, 0, 2)
        return spatial_layout(out, row_count, col_count)
    devices = row_devices * col_devices
    row_fold, col_fold = WIN // row_devices, WIN // col_devices
    row_rest, col_rest = row_count // row_fold, col_count // col_fold
    parts = row_rest // WIN
    count = WIN * col_rest // devices
    pieces = col_rest // count
    order = np.arange(WIN * WIN).reshape(row_devices, col_devices, row_fold, col_fold)
    at = np.indices(order.shape).reshape(4, -1)
    grid_bias = key_major_bias(grid_table, at[0] * row_fold + at[2], at[1] * col_fold + at[3])
    strips = conv_out.reshape(row_fold, parts, WIN, col_count, feats)
    results = []
    for part in range(parts):
        section = run_block(
            strips[:, part].reshape(-1, feats), ("blocks", col_count), block_bias
        )
        sent = (
            section.reshape(row_fold, WIN, col_fold, pieces, count, feats)
            .transpose(1, 3, 0, 2, 4, 5)
            .reshape(devices, row_fold * col_fold * count, feats)
        )
        got = lax.all_to_all(sent, ("row", "col"), split_axis=0, concat_axis=0, tiled=True)
        out = run_grid(got.reshape(-1, feats), ("strided", count), grid_bias)
        back = lax.all_to_all(
            out.reshape(devices, -1, feats), ("row", "col"), split_axis=0, concat_axis=0, tiled=True
        )
        results.append(
            back.reshape(WIN, pieces, row_fold, col_fold, count, feats)
            .transpose(2, 0, 3, 1, 4, 5)
            .reshape(row_fold, WIN, col_count, feats)
        )
    return jnp.stack(results, axis=1).reshape(row_count, col_count, feats)


def per_device(
    latent,
    conv_scale,
    conv_shift,
    expand_weight,
    depth_kernel,
    squeeze_down,
    squeeze_up,
    project_weight,
    block_gain,
    block_projection,
    block_output,
    block_table,
    first_gain,
    first_expand,
    first_reduce,
    grid_gain,
    grid_projection,
    grid_output,
    grid_table,
    second_gain,
    second_expand,
    second_reduce,
):
    row_devices = lax.axis_size("row")
    col_devices = lax.axis_size("col")
    row_count, col_count, channels = latent.shape
    conv_in = (latent.astype(jnp.float32) * conv_scale + conv_shift).astype(jnp.bfloat16)
    expanded = jax.nn.gelu(
        jnp.dot(conv_in, expand_weight, preferred_element_type=jnp.float32), approximate=True
    ).astype(jnp.bfloat16)
    padded = extended(expanded, (("row", 0), ("col", 1)), 1)
    summed = jnp.zeros((row_count, col_count, padded.shape[-1]), jnp.float32)
    for offset in range(9):
        down_step = offset // 3
        side_step = offset % 3
        summed = (
            summed
            + padded[down_step : down_step + row_count, side_step : side_step + col_count].astype(
                jnp.float32
            )
            * depth_kernel[offset]
        )
    depthwise = jax.nn.gelu(summed, approximate=True)
    local_sums = jnp.sum(depthwise, axis=(0, 1)).reshape(-1, 128)
    channel_sums = axis_sum(axis_sum(local_sums, "row", 1), "col", 2).reshape(-1)
    pooled = channel_sums / (row_count * row_devices * col_count * col_devices)
    excite = squeeze_gate(pooled, squeeze_down, squeeze_up)
    gated = (depthwise * excite).astype(jnp.bfloat16)
    conv_out = (
        latent.astype(jnp.float32)
        + jnp.dot(gated, project_weight, preferred_element_type=jnp.float32)
    ).astype(jnp.bfloat16)

    def run_block(cells, layout, bias):
        return mixer(
            cells, layout, block_gain, block_projection, block_output, bias, first_gain,
            first_expand, first_reduce, block_table.shape[0],
        )

    def run_grid(cells, layout, bias):
        return mixer(
            cells, layout, grid_gain, grid_projection, grid_output, bias, second_gain,
            second_expand, second_reduce, grid_table.shape[0],
        )

    return split_sublayers(conv_out, run_block, run_grid, block_table, grid_table)


def solution(mesh):
    placed = (
        P("row", "col", None),
        P(),
        P(),
        P(),
        P(),
        P(),
        P(),
        P(),
        P(),
        P(),
        P(),
        P(),
        P(),
        P(),
        P(),
        P(),
        P(),
        P(),
        P(),
        P(),
        P(),
        P(),
    )
    return jax.shard_map(
        per_device, mesh=mesh, in_specs=placed, out_specs=P("row", "col", None), check_vma=False
    )
```

```python
import functools

import jax
import jax.numpy as jnp
import numpy as np
from jax import lax
from jax.experimental import pallas as pl
from jax.experimental.pallas import tpu as pltpu
from jax.sharding import PartitionSpec as P

WIN = 8


def extended(cells, sides, width):
    for axis, dim in sides:
        count = lax.axis_size(axis)
        ends = count - 1
        head = lax.slice_in_dim(cells, 0, width, axis=dim)
        tail = lax.slice_in_dim(cells, cells.shape[dim] - width, cells.shape[dim], axis=dim)
        cells = jnp.concatenate(
            [
                lax.ppermute(tail, axis, [(i, (i + 1) % count) for i in range(ends)]),
                cells,
                lax.ppermute(head, axis, [((i + 1) % count, i) for i in range(ends)]),
            ],
            axis=dim,
        )
    return cells


def layer_norm_apply(values, norm_gain):
    widened = values.astype(jnp.float32)
    center = widened - jnp.mean(widened, axis=-1, keepdims=True)
    spread = jnp.mean(center * center, axis=-1, keepdims=True)
    return (center * lax.rsqrt(spread + 1e-05) * norm_gain).astype(jnp.bfloat16)


def position_bias(offset_bias_lookup):
    spots = offset_bias_lookup.shape[1]
    position = jnp.arange(WIN * WIN)
    down_pos = position // WIN
    across = position % WIN
    relative = (down_pos[:, None] - down_pos[None, :] + WIN - 1) * (2 * WIN - 1) + (
        across[:, None] - across[None, :] + WIN - 1
    )
    indicator_matrix = (relative[:, :, None] == jnp.arange(spots)[None, None, :]).astype(
        jnp.float32
    )
    return jnp.einsum(
        "bp,rjp->brj", offset_bias_lookup, indicator_matrix, precision=lax.Precision.HIGHEST
    )


def attend(triple, pos_bias):
    window_count, tokens, three_width = triple.shape
    feature_width = three_width // 3
    head_count = pos_bias.shape[0]
    head_size = feature_width // head_count
    queries = triple[..., :feature_width].reshape(window_count, tokens, head_count, head_size)
    key_row_list = triple[..., feature_width : 2 * feature_width].reshape(
        window_count, tokens, head_count, head_size
    )
    values = triple[..., 2 * feature_width :].reshape(window_count, tokens, head_count, head_size)
    scores = (
        jnp.einsum("nqhd,nkhd->nhqk", queries, key_row_list, preferred_element_type=jnp.float32)
        * head_size ** (-0.5)
        + pos_bias[None]
    )
    row_max = jnp.max(scores, axis=-1, keepdims=True)
    weight_tensors = jnp.exp(scores - row_max)
    attention_weight_map = (
        weight_tensors / jnp.sum(weight_tensors, axis=-1, keepdims=True)
    ).astype(jnp.bfloat16)
    mixed = jnp.einsum(
        "nhqk,nkhd->nqhd", attention_weight_map, values, preferred_element_type=jnp.float32
    )
    return mixed.astype(jnp.bfloat16).reshape(window_count, tokens, feature_width)


def attention_sublayer(windows, norm_gain, in_weight, out_weight, pos_bias):
    normed = layer_norm_apply(windows, norm_gain)
    triple = jnp.dot(normed, in_weight, preferred_element_type=jnp.float32).astype(jnp.bfloat16)
    mixed = attend(triple, pos_bias)
    return (
        windows.astype(jnp.float32) + jnp.dot(mixed, out_weight, preferred_element_type=jnp.float32)
    ).astype(jnp.bfloat16)


def feed_forward(values, norm_gain, in_weight, out_weight):
    normed = layer_norm_apply(values, norm_gain)
    hidden = jax.nn.gelu(
        jnp.dot(normed, in_weight, preferred_element_type=jnp.float32), approximate=True
    ).astype(jnp.bfloat16)
    return (
        values.astype(jnp.float32) + jnp.dot(hidden, out_weight, preferred_element_type=jnp.float32)
    ).astype(jnp.bfloat16)


def to_blocks(field):
    row_count, col_count, feats = field.shape
    return (
        field.reshape(row_count // WIN, WIN, col_count // WIN, WIN, feats)
        .transpose(0, 2, 1, 3, 4)
        .reshape(-1, WIN * WIN, feats)
    )


def from_blocks(windows, row_count, col_count):
    feats = windows.shape[-1]
    return (
        windows.reshape(row_count // WIN, col_count // WIN, WIN, WIN, feats)
        .transpose(0, 2, 1, 3, 4)
        .reshape(row_count, col_count, feats)
    )


def axis_shape(length, devices):
    fold = max(1, WIN // devices)
    rest = length // max(devices, WIN)
    span = min(devices, WIN)
    return (fold, rest, span, devices // span)


def grid_layout(field):
    row_devices = lax.axis_size("row")
    col_devices = lax.axis_size("col")
    row_count, col_count, feats = field.shape
    row_fold, row_rest, row_span, row_hop = axis_shape(row_count, row_devices)
    col_fold, col_rest, col_span, col_hop = axis_shape(col_count, col_devices)
    ordered_layout = field.reshape(
        row_fold, row_devices, row_rest, col_fold, col_devices, col_rest, feats
    )
    flat = ordered_layout.transpose(1, 4, 0, 2, 3, 5, 6).reshape(
        row_devices * col_devices, row_fold, row_rest, col_fold, col_rest, feats
    )
    flat = lax.all_to_all(flat, ("row", "col"), split_axis=0, concat_axis=0, tiled=True)
    moved = flat.reshape(
        row_devices, col_devices, row_fold, row_rest, col_fold, col_rest, feats
    ).transpose(2, 0, 3, 4, 1, 5, 6)
    moved = moved.reshape(
        row_fold, row_span, row_hop, row_rest, col_fold, col_span, col_hop, col_rest, feats
    )
    return moved.transpose(2, 3, 6, 7, 1, 0, 5, 4, 8).reshape(-1, WIN * WIN, feats)


def spatial_layout(windows, row_count, col_count):
    row_devices = lax.axis_size("row")
    col_devices = lax.axis_size("col")
    feats = windows.shape[-1]
    row_fold, row_rest, row_span, row_hop = axis_shape(row_count, row_devices)
    col_fold, col_rest, col_span, col_hop = axis_shape(col_count, col_devices)
    gridded = windows.reshape(
        row_hop, row_rest, col_hop, col_rest, row_span, row_fold, col_span, col_fold, feats
    )
    ordered_layout = gridded.transpose(5, 4, 0, 1, 7, 6, 2, 3, 8).reshape(
        row_fold, row_devices, row_rest, col_fold, col_devices, col_rest, feats
    )
    flat = ordered_layout.transpose(1, 4, 0, 2, 3, 5, 6).reshape(
        row_devices * col_devices, row_fold, row_rest, col_fold, col_rest, feats
    )
    flat = lax.all_to_all(flat, ("row", "col"), split_axis=0, concat_axis=0, tiled=True)
    moved = flat.reshape(
        row_devices, col_devices, row_fold, row_rest, col_fold, col_rest, feats
    ).transpose(2, 0, 3, 4, 1, 5, 6)
    return moved.reshape(row_count, col_count, feats)


def squeeze_gate(pooled, squeeze_down, squeeze_up):
    reduced = jax.nn.silu(
        jnp.dot(pooled[None, :], squeeze_down.astype(jnp.float32), precision=lax.Precision.HIGHEST)
    )
    return jax.nn.sigmoid(
        jnp.dot(reduced, squeeze_up.astype(jnp.float32), precision=lax.Precision.HIGHEST)
    )[0]


def axis_sum_kernel(axis, count, x_ref, o_ref, slots, send_sem, recv_sem):
    me = lax.axis_index(axis)
    barrier = pltpu.get_barrier_semaphore()
    peers = [lax.rem(me + step, count) for step in range(1, count)]
    for peer in peers:
        pl.semaphore_signal(
            barrier, inc=1, device_id={axis: peer}, device_id_type=pl.DeviceIdType.MESH
        )
    pl.semaphore_wait(barrier, count - 1)
    copies = []
    for step, peer in enumerate(peers):
        copy = pltpu.make_async_remote_copy(
            src_ref=x_ref,
            dst_ref=slots.at[step],
            send_sem=send_sem.at[step],
            recv_sem=recv_sem.at[step],
            device_id={axis: peer},
            device_id_type=pl.DeviceIdType.MESH,
        )
        copy.start()
        copies.append(copy)
    for copy in copies:
        copy.wait()
    total = x_ref[...]
    for step in range(count - 1):
        total = total + slots[step]
    o_ref[...] = total


def axis_sum(values, axis, collective_id):
    count = lax.axis_size(axis)
    if count == 1:
        return values
    return pl.pallas_call(
        functools.partial(axis_sum_kernel, axis, count),
        out_shape=jax.ShapeDtypeStruct(values.shape, values.dtype),
        in_specs=[pl.BlockSpec(memory_space=pltpu.VMEM)],
        out_specs=pl.BlockSpec(memory_space=pltpu.VMEM),
        scratch_shapes=[
            pltpu.VMEM((count - 1,) + values.shape, values.dtype),
            pltpu.SemaphoreType.DMA((count - 1,)),
            pltpu.SemaphoreType.DMA((count - 1,)),
        ],
        compiler_params=pltpu.CompilerParams(collective_id=collective_id, has_side_effects=True),
        name="axis_sum_" + axis,
    )(values)


LANES = 128
GROUP = 256


def normed_rows(widened, gain):
    center = widened - jnp.mean(widened, axis=-1, keepdims=True)
    spread = jnp.mean(center * center, axis=-1, keepdims=True)
    return (center * lax.rsqrt(spread + 1e-05) * gain).astype(jnp.bfloat16)


def mixer_kernel(
    layout, head_size, x_ref, gain_ref, bias_ref, late_gain_ref, proj_hbm, out_hbm, up_hbm, down_hbm,
    o_ref, triple, heads, proj_ref, out_w_ref, up_ref, down_ref, sems,
):
    kind, across = layout
    rows_total, feats = x_ref.shape
    tokens = WIN * WIN
    window_count = rows_total // tokens
    slabs = feats // LANES
    per_slab = LANES // head_size
    moves = [
        pltpu.make_async_copy(src, dst, sems.at[k])
        for k, (src, dst) in enumerate(
            ((proj_hbm, proj_ref), (out_hbm, out_w_ref), (up_hbm, up_ref), (down_hbm, down_ref))
        )
    ]
    for move in moves:
        move.start()
    moves[0].wait()
    chunk = 256

    def project(step, carry):
        rows = pl.ds(pl.multiple_of(step * chunk, chunk), chunk)
        normed = normed_rows(x_ref[rows, :].astype(jnp.float32), gain_ref[...])
        for part in range(3 * slabs // 2):
            product = jnp.dot(
                normed, proj_ref[:, part * GROUP : (part + 1) * GROUP],
                preferred_element_type=jnp.float32,
            ).astype(jnp.bfloat16).astype(jnp.float32)
            triple[2 * part, rows, :] = product[:, :LANES]
            triple[2 * part + 1, rows, :] = product[:, LANES:]
        return carry

    lax.fori_loop(0, rows_total // chunk, project, 0)

    def places(window):
        if kind == "strided":
            return [pl.ds(window, tokens, stride=across)]
        per_row = across // WIN
        base = (window // per_row) * (WIN * across) + (window % per_row) * WIN
        return [pl.ds(pl.multiple_of(base + r * across, WIN), WIN) for r in range(WIN)]

    lane = lax.broadcasted_iota(jnp.int32, (tokens, GROUP), 1)
    head_of = (lane % LANES) // head_size
    scale = head_size ** (-0.5)

    def one_window(window):
        spots = places(window)

        def fetch(slab):
            pieces = [triple[slab, spot, :] for spot in spots]
            whole = pieces[0] if len(pieces) == 1 else jnp.concatenate(pieces, axis=0)
            return whole

        empty = jnp.zeros((tokens, LANES), jnp.bfloat16)
        for group in range(slabs // 2):
            first, second = 2 * group, 2 * group + 1
            query_0 = fetch(first).astype(jnp.bfloat16)
            query_1 = fetch(second).astype(jnp.bfloat16)
            keys = jnp.concatenate([fetch(slabs + first), fetch(slabs + second)], axis=1)
            vals = jnp.concatenate([fetch(2 * slabs + first), fetch(2 * slabs + second)], axis=1)
            block_q = jnp.concatenate(
                [
                    jnp.concatenate([query_0, empty], axis=1),
                    jnp.concatenate([empty, query_1], axis=1),
                ],
                axis=0,
            )
            block_k = jnp.concatenate(
                [jnp.where(head_of == j, keys, 0.0).astype(jnp.bfloat16) for j in range(per_slab)],
                axis=0,
            )
            block_v = jnp.concatenate(
                [jnp.where(head_of == j, vals, 0.0).astype(jnp.bfloat16) for j in range(per_slab)],
                axis=0,
            )
            scores = lax.dot_general(
                block_k, block_q, (((1,), (1,)), ((), ())), preferred_element_type=jnp.float32
            )
            scores = (scores * scale + bias_ref[group]).reshape(per_slab, tokens, 2 * tokens)
            weights = jnp.exp(scores - jnp.max(scores, axis=1, keepdims=True))
            shares = weights / jnp.sum(weights, axis=1, keepdims=True)
            shares = shares.reshape(per_slab * tokens, 2 * tokens).astype(jnp.bfloat16)
            mixed = lax.dot_general(
                shares, block_v, (((0,), (0,)), ((), ())), preferred_element_type=jnp.float32
            )
            for slab, part in (
                (first, mixed[:tokens, :LANES]), (second, mixed[tokens:, LANES:])
            ):
                if len(spots) == 1:
                    heads[slab, spots[0], :] = part
                else:
                    for r, spot in enumerate(spots):
                        heads[slab, spot, :] = part[r * WIN : (r + 1) * WIN]

    def attend_pair(step, carry):
        one_window(2 * step)
        one_window(2 * step + 1)
        return carry

    lax.fori_loop(0, window_count // 2, attend_pair, 0)
    for move in moves[1:]:
        move.wait()
    hidden_width = up_ref.shape[1]
    tile = 512

    def feed(step, carry):
        rows = pl.ds(pl.multiple_of(step * chunk, chunk), chunk)
        mixed = jnp.concatenate([heads[s, rows, :] for s in range(slabs)], axis=1).astype(jnp.bfloat16)
        value = (
            x_ref[rows, :].astype(jnp.float32)
            + jnp.dot(mixed, out_w_ref[...], preferred_element_type=jnp.float32)
        ).astype(jnp.bfloat16).astype(jnp.float32)
        normed = normed_rows(value, late_gain_ref[...])
        for k in range(hidden_width // tile):
            part = slice(k * tile, (k + 1) * tile)
            hidden = jax.nn.gelu(
                jnp.dot(normed, up_ref[:, part], preferred_element_type=jnp.float32),
                approximate=True,
            ).astype(jnp.bfloat16)
            value = value + jnp.dot(hidden, down_ref[part, :], preferred_element_type=jnp.float32)
        o_ref[rows, :] = value.astype(jnp.bfloat16)
        return carry

    lax.fori_loop(0, rows_total // chunk, feed, 0)


def mixer(x, layout, gain, in_weight, out_weight, bias, late_gain, up, down, heads_count):
    rows, feats = x.shape
    vmem = pl.BlockSpec(memory_space=pltpu.VMEM)
    hbm = pl.BlockSpec(memory_space=pltpu.HBM)
    flops = 8 * rows * feats * (4 * feats + 2 * up.shape[1])
    return pl.pallas_call(
        functools.partial(mixer_kernel, layout, feats // heads_count),
        out_shape=jax.ShapeDtypeStruct((rows, feats), jnp.bfloat16),
        in_specs=[vmem] * 4 + [hbm] * 4,
        out_specs=vmem,
        scratch_shapes=[
            pltpu.VMEM((3 * feats // LANES, rows, LANES), jnp.float32),
            pltpu.VMEM((feats // LANES, rows, LANES), jnp.float32),
            pltpu.VMEM(in_weight.shape, jnp.bfloat16),
            pltpu.VMEM(out_weight.shape, jnp.bfloat16),
            pltpu.VMEM(up.shape, jnp.bfloat16),
            pltpu.VMEM(down.shape, jnp.bfloat16),
            pltpu.SemaphoreType.DMA((4,)),
        ],
        compiler_params=pltpu.CompilerParams(vmem_limit_bytes=60 * 1024 * 1024),
        cost_estimate=pl.CostEstimate(
            flops=flops, bytes_accessed=12 * 1024 * 1024, transcendentals=0
        ),
        name="mixer_" + layout[0],
    )(x, gain[None], bias, late_gain[None], in_weight, out_weight, up, down)


def key_major_bias(table, down, across):
    head_count, spots = table.shape
    relative = (down[None, :] - down[:, None] + WIN - 1) * (2 * WIN - 1) + (
        across[None, :] - across[:, None] + WIN - 1
    )
    tokens = WIN * WIN
    chosen = (jnp.arange(spots)[:, None] == jnp.asarray(relative.reshape(-1))[None, :]).astype(
        jnp.float32
    )
    spread = jnp.dot(table, chosen, precision=lax.Precision.HIGHEST)
    return (
        spread.reshape(head_count // 8, 2, 4, tokens, tokens)
        .transpose(0, 2, 3, 1, 4)
        .reshape(head_count // 8, 4 * tokens, 2 * tokens)
    )


def split_sublayers(conv_out, run_block, run_grid, block_table, grid_table):
    row_devices = lax.axis_size("row")
    col_devices = lax.axis_size("col")
    row_count, col_count, feats = conv_out.shape
    plain = np.arange(WIN * WIN)
    block_bias = key_major_bias(block_table, plain // WIN, plain % WIN)
    if row_devices > WIN or col_devices > WIN:
        section = run_block(conv_out.reshape(-1, feats), ("blocks", col_count), block_bias)
        windows = grid_layout(section.reshape(row_count, col_count, feats))
        count = windows.shape[0]
        bias = key_major_bias(grid_table, plain // WIN, plain % WIN)
        out = run_grid(windows.transpose(1, 0, 2).reshape(-1, feats), ("strided", count), bias)
        out = out.reshape(WIN * WIN, count, feats).transpose(1, 0, 2)
        return spatial_layout(out, row_count, col_count)
    devices = row_devices * col_devices
    row_fold, col_fold = WIN // row_devices, WIN // col_devices
    row_rest, col_rest = row_count // row_fold, col_count // col_fold
    parts = row_rest // WIN
    count = WIN * col_rest // devices
    pieces = col_rest // count
    order = np.arange(WIN * WIN).reshape(row_devices, col_devices, row_fold, col_fold)
    at = np.indices(order.shape).reshape(4, -1)
    grid_bias = key_major_bias(grid_table, at[0] * row_fold + at[2], at[1] * col_fold + at[3])
    strips = conv_out.reshape(row_fold, parts, WIN, col_count, feats)
    results = []
    for part in range(parts):
        section = run_block(
            strips[:, part].reshape(-1, feats), ("blocks", col_count), block_bias
        )
        sent = (
            section.reshape(row_fold, WIN, col_fold, pieces, count, feats)
            .transpose(1, 3, 0, 2, 4, 5)
            .reshape(devices, row_fold * col_fold * count, feats)
        )
        got = lax.all_to_all(sent, ("row", "col"), split_axis=0, concat_axis=0, tiled=True)
        out = run_grid(got.reshape(-1, feats), ("strided", count), grid_bias)
        back = lax.all_to_all(
            out.reshape(devices, -1, feats), ("row", "col"), split_axis=0, concat_axis=0, tiled=True
        )
        results.append(
            back.reshape(WIN, pieces, row_fold, col_fold, count, feats)
            .transpose(2, 0, 3, 1, 4, 5)
            .reshape(row_fold, WIN, col_count, feats)
        )
    return jnp.stack(results, axis=1).reshape(row_count, col_count, feats)


PAD = 8


def conv_kernel(
    row_count, col_count, flags, ext_ref, scale_ref, shift_ref, expand_ref, taps_ref,
    o_ref, sums_ref, conv_in, expanded,
):
    wide = col_count + PAD
    tall = row_count + 2
    width = expand_ref.shape[1]
    block = expanded.shape[-1]
    bounds = [8 * k for k in range(row_count // 8)] + [tall]
    for low, high in zip(bounds[:-1], bounds[1:]):
        rows = slice(low * wide, high * wide)
        conv_in[rows, :] = (
            ext_ref[rows, :].astype(jnp.float32) * scale_ref[...] + shift_ref[...]
        ).astype(jnp.bfloat16)
    spot = lax.broadcasted_iota(jnp.int32, (1, PAD, block), 1)
    side = jnp.where(spot == 0, flags[3], jnp.where(spot == PAD - 1, flags[2], 0.0))

    def channels(step, carry):
        lanes = pl.ds(pl.multiple_of(step * block, block), block)
        for low, high in zip(bounds[:-1], bounds[1:]):
            product = jnp.dot(
                conv_in[low * wide : high * wide, :], expand_ref[:, lanes],
                preferred_element_type=jnp.float32,
            )
            value = jax.nn.gelu(product, approximate=True).astype(jnp.bfloat16)
            expanded[low:high] = value.astype(jnp.float32).reshape(high - low, wide, block)
        expanded[0] = expanded[0] * flags[0]
        expanded[tall - 1] = expanded[tall - 1] * flags[1]
        expanded[:, col_count:, :] = expanded[:, col_count:, :] * side
        for half in range(block // LANES):
            inner = slice(half * LANES, (half + 1) * LANES)
            outer = pl.ds(pl.multiple_of(step * block + half * LANES, LANES), LANES)
            taps = [taps_ref[k : k + 1, outer] for k in range(9)]

            def rows_of(group, total):
                base = group * 4
                held = [expanded[base + k, :, inner] for k in range(6)]
                for k in range(4):
                    parts = [
                        held[k] * taps[side_step]
                        + held[k + 1] * taps[3 + side_step]
                        + held[k + 2] * taps[6 + side_step]
                        for side_step in range(3)
                    ]
                    summed = (
                        pltpu.roll(parts[0], 1, 0) + parts[1] + pltpu.roll(parts[2], wide - 1, 0)
                    )[:col_count]
                    deep = jax.nn.gelu(summed, approximate=True)
                    total = total + jnp.sum(deep.reshape(col_count // 8, 8, LANES), axis=0)
                    at = pl.ds(pl.multiple_of((base + k) * col_count, col_count), col_count)
                    o_ref[at, outer] = deep.astype(o_ref.dtype)
                return total

            total = lax.fori_loop(0, row_count // 4, rows_of, jnp.zeros((8, LANES), jnp.float32))
            sums_ref[:, outer] = jnp.sum(total, axis=0, keepdims=True)
        return carry

    lax.fori_loop(0, width // block, channels, 0)


def depthwise_stage(latent, conv_scale, conv_shift, expand_weight, depth_kernel):
    row_count, col_count, feats = latent.shape
    width = expand_weight.shape[1]
    row_at, col_at = lax.axis_index("row"), lax.axis_index("col")
    flags = jnp.stack(
        [row_at > 0, row_at < lax.axis_size("row") - 1, col_at > 0, col_at < lax.axis_size("col") - 1]
    ).astype(jnp.float32)
    tall = extended(latent, (("row", 0),), 1)
    count = lax.axis_size("col")
    ahead = [(i, i + 1) for i in range(count - 1)]
    left = lax.ppermute(tall[:, col_count - 1 :], "col", ahead)
    right = lax.ppermute(tall[:, :1], "col", [(b, a) for a, b in ahead])
    blank = jnp.zeros((row_count + 2, PAD - 2, feats), latent.dtype)
    ext = jnp.concatenate([tall, right, blank, left], axis=1).reshape(-1, feats)
    vmem = pl.BlockSpec(memory_space=pltpu.VMEM)
    block = 256
    return pl.pallas_call(
        functools.partial(conv_kernel, row_count, col_count),
        out_shape=(
            jax.ShapeDtypeStruct((row_count * col_count, width), jnp.bfloat16),
            jax.ShapeDtypeStruct((1, width), jnp.float32),
        ),
        in_specs=[pl.BlockSpec(memory_space=pltpu.SMEM)] + [vmem] * 5,
        out_specs=(vmem, vmem),
        scratch_shapes=[
            pltpu.VMEM(ext.shape, jnp.bfloat16),
            pltpu.VMEM((row_count + 2, col_count + PAD, block), jnp.float32),
        ],
        compiler_params=pltpu.CompilerParams(vmem_limit_bytes=40 * 1024 * 1024),
        name="conv_stage",
    )(flags, ext, conv_scale[None], conv_shift[None], expand_weight, depth_kernel)


def per_device(
    latent,
    conv_scale,
    conv_shift,
    expand_weight,
    depth_kernel,
    squeeze_down,
    squeeze_up,
    project_weight,
    block_gain,
    block_projection,
    block_output,
    block_table,
    first_gain,
    first_expand,
    first_reduce,
    grid_gain,
    grid_projection,
    grid_output,
    grid_table,
    second_gain,
    second_expand,
    second_reduce,
):
    row_devices = lax.axis_size("row")
    col_devices = lax.axis_size("col")
    row_count, col_count, channels = latent.shape
    depthwise, local_sums = depthwise_stage(
        latent, conv_scale, conv_shift, expand_weight, depth_kernel
    )
    local_sums = local_sums.reshape(-1, LANES)
    channel_sums = axis_sum(axis_sum(local_sums, "row", 1), "col", 2).reshape(-1)
    pooled = channel_sums / (row_count * row_devices * col_count * col_devices)
    excite = squeeze_gate(pooled, squeeze_down, squeeze_up)
    gated = (depthwise.astype(jnp.float32) * excite).astype(jnp.bfloat16)
    conv_out = (
        latent.reshape(-1, channels).astype(jnp.float32)
        + jnp.dot(gated, project_weight, preferred_element_type=jnp.float32)
    ).astype(jnp.bfloat16).reshape(row_count, col_count, channels)

    def run_block(cells, layout, bias):
        return mixer(
            cells, layout, block_gain, block_projection, block_output, bias, first_gain,
            first_expand, first_reduce, block_table.shape[0],
        )

    def run_grid(cells, layout, bias):
        return mixer(
            cells, layout, grid_gain, grid_projection, grid_output, bias, second_gain,
            second_expand, second_reduce, grid_table.shape[0],
        )

    return split_sublayers(conv_out, run_block, run_grid, block_table, grid_table)


def solution(mesh):
    placed = (
        P("row", "col", None),
        P(),
        P(),
        P(),
        P(),
        P(),
        P(),
        P(),
        P(),
        P(),
        P(),
        P(),
        P(),
        P(),
        P(),
        P(),
        P(),
        P(),
        P(),
        P(),
        P(),
        P(),
    )
    return jax.shard_map(
        per_device, mesh=mesh, in_specs=placed, out_specs=P("row", "col", None), check_vma=False
    )
```

```python
import functools

import jax
import jax.numpy as jnp
import numpy as np
from jax import lax
from jax.experimental import pallas as pl
from jax.experimental.pallas import tpu as pltpu
from jax.sharding import PartitionSpec as P

WIN = 8


def extended(cells, sides, width):
    for axis, dim in sides:
        count = lax.axis_size(axis)
        ends = count - 1
        head = lax.slice_in_dim(cells, 0, width, axis=dim)
        tail = lax.slice_in_dim(cells, cells.shape[dim] - width, cells.shape[dim], axis=dim)
        cells = jnp.concatenate(
            [
                lax.ppermute(tail, axis, [(i, (i + 1) % count) for i in range(ends)]),
                cells,
                lax.ppermute(head, axis, [((i + 1) % count, i) for i in range(ends)]),
            ],
            axis=dim,
        )
    return cells


def layer_norm_apply(values, norm_gain):
    widened = values.astype(jnp.float32)
    center = widened - jnp.mean(widened, axis=-1, keepdims=True)
    spread = jnp.mean(center * center, axis=-1, keepdims=True)
    return (center * lax.rsqrt(spread + 1e-05) * norm_gain).astype(jnp.bfloat16)


def position_bias(offset_bias_lookup):
    spots = offset_bias_lookup.shape[1]
    position = jnp.arange(WIN * WIN)
    down_pos = position // WIN
    across = position % WIN
    relative = (down_pos[:, None] - down_pos[None, :] + WIN - 1) * (2 * WIN - 1) + (
        across[:, None] - across[None, :] + WIN - 1
    )
    indicator_matrix = (relative[:, :, None] == jnp.arange(spots)[None, None, :]).astype(
        jnp.float32
    )
    return jnp.einsum(
        "bp,rjp->brj", offset_bias_lookup, indicator_matrix, precision=lax.Precision.HIGHEST
    )


def attend(triple, pos_bias):
    window_count, tokens, three_width = triple.shape
    feature_width = three_width // 3
    head_count = pos_bias.shape[0]
    head_size = feature_width // head_count
    queries = triple[..., :feature_width].reshape(window_count, tokens, head_count, head_size)
    key_row_list = triple[..., feature_width : 2 * feature_width].reshape(
        window_count, tokens, head_count, head_size
    )
    values = triple[..., 2 * feature_width :].reshape(window_count, tokens, head_count, head_size)
    scores = (
        jnp.einsum("nqhd,nkhd->nhqk", queries, key_row_list, preferred_element_type=jnp.float32)
        * head_size ** (-0.5)
        + pos_bias[None]
    )
    row_max = jnp.max(scores, axis=-1, keepdims=True)
    weight_tensors = jnp.exp(scores - row_max)
    attention_weight_map = (
        weight_tensors / jnp.sum(weight_tensors, axis=-1, keepdims=True)
    ).astype(jnp.bfloat16)
    mixed = jnp.einsum(
        "nhqk,nkhd->nqhd", attention_weight_map, values, preferred_element_type=jnp.float32
    )
    return mixed.astype(jnp.bfloat16).reshape(window_count, tokens, feature_width)


def attention_sublayer(windows, norm_gain, in_weight, out_weight, pos_bias):
    normed = layer_norm_apply(windows, norm_gain)
    triple = jnp.dot(normed, in_weight, preferred_element_type=jnp.float32).astype(jnp.bfloat16)
    mixed = attend(triple, pos_bias)
    return (
        windows.astype(jnp.float32) + jnp.dot(mixed, out_weight, preferred_element_type=jnp.float32)
    ).astype(jnp.bfloat16)


def feed_forward(values, norm_gain, in_weight, out_weight):
    normed = layer_norm_apply(values, norm_gain)
    hidden = jax.nn.gelu(
        jnp.dot(normed, in_weight, preferred_element_type=jnp.float32), approximate=True
    ).astype(jnp.bfloat16)
    return (
        values.astype(jnp.float32) + jnp.dot(hidden, out_weight, preferred_element_type=jnp.float32)
    ).astype(jnp.bfloat16)


def to_blocks(field):
    row_count, col_count, feats = field.shape
    return (
        field.reshape(row_count // WIN, WIN, col_count // WIN, WIN, feats)
        .transpose(0, 2, 1, 3, 4)
        .reshape(-1, WIN * WIN, feats)
    )


def from_blocks(windows, row_count, col_count):
    feats = windows.shape[-1]
    return (
        windows.reshape(row_count // WIN, col_count // WIN, WIN, WIN, feats)
        .transpose(0, 2, 1, 3, 4)
        .reshape(row_count, col_count, feats)
    )


def axis_shape(length, devices):
    fold = max(1, WIN // devices)
    rest = length // max(devices, WIN)
    span = min(devices, WIN)
    return (fold, rest, span, devices // span)


def grid_layout(field):
    row_devices = lax.axis_size("row")
    col_devices = lax.axis_size("col")
    row_count, col_count, feats = field.shape
    row_fold, row_rest, row_span, row_hop = axis_shape(row_count, row_devices)
    col_fold, col_rest, col_span, col_hop = axis_shape(col_count, col_devices)
    ordered_layout = field.reshape(
        row_fold, row_devices, row_rest, col_fold, col_devices, col_rest, feats
    )
    flat = ordered_layout.transpose(1, 4, 0, 2, 3, 5, 6).reshape(
        row_devices * col_devices, row_fold, row_rest, col_fold, col_rest, feats
    )
    flat = lax.all_to_all(flat, ("row", "col"), split_axis=0, concat_axis=0, tiled=True)
    moved = flat.reshape(
        row_devices, col_devices, row_fold, row_rest, col_fold, col_rest, feats
    ).transpose(2, 0, 3, 4, 1, 5, 6)
    moved = moved.reshape(
        row_fold, row_span, row_hop, row_rest, col_fold, col_span, col_hop, col_rest, feats
    )
    return moved.transpose(2, 3, 6, 7, 1, 0, 5, 4, 8).reshape(-1, WIN * WIN, feats)


def spatial_layout(windows, row_count, col_count):
    row_devices = lax.axis_size("row")
    col_devices = lax.axis_size("col")
    feats = windows.shape[-1]
    row_fold, row_rest, row_span, row_hop = axis_shape(row_count, row_devices)
    col_fold, col_rest, col_span, col_hop = axis_shape(col_count, col_devices)
    gridded = windows.reshape(
        row_hop, row_rest, col_hop, col_rest, row_span, row_fold, col_span, col_fold, feats
    )
    ordered_layout = gridded.transpose(5, 4, 0, 1, 7, 6, 2, 3, 8).reshape(
        row_fold, row_devices, row_rest, col_fold, col_devices, col_rest, feats
    )
    flat = ordered_layout.transpose(1, 4, 0, 2, 3, 5, 6).reshape(
        row_devices * col_devices, row_fold, row_rest, col_fold, col_rest, feats
    )
    flat = lax.all_to_all(flat, ("row", "col"), split_axis=0, concat_axis=0, tiled=True)
    moved = flat.reshape(
        row_devices, col_devices, row_fold, row_rest, col_fold, col_rest, feats
    ).transpose(2, 0, 3, 4, 1, 5, 6)
    return moved.reshape(row_count, col_count, feats)


def squeeze_gate(pooled, squeeze_down, squeeze_up):
    reduced = jax.nn.silu(
        jnp.dot(pooled[None, :], squeeze_down.astype(jnp.float32), precision=lax.Precision.HIGHEST)
    )
    return jax.nn.sigmoid(
        jnp.dot(reduced, squeeze_up.astype(jnp.float32), precision=lax.Precision.HIGHEST)
    )[0]


def axis_sum_kernel(axis, count, x_ref, o_ref, slots, send_sem, recv_sem):
    me = lax.axis_index(axis)
    barrier = pltpu.get_barrier_semaphore()
    peers = [lax.rem(me + step, count) for step in range(1, count)]
    for peer in peers:
        pl.semaphore_signal(
            barrier, inc=1, device_id={axis: peer}, device_id_type=pl.DeviceIdType.MESH
        )
    pl.semaphore_wait(barrier, count - 1)
    copies = []
    for step, peer in enumerate(peers):
        copy = pltpu.make_async_remote_copy(
            src_ref=x_ref,
            dst_ref=slots.at[step],
            send_sem=send_sem.at[step],
            recv_sem=recv_sem.at[step],
            device_id={axis: peer},
            device_id_type=pl.DeviceIdType.MESH,
        )
        copy.start()
        copies.append(copy)
    for copy in copies:
        copy.wait()
    total = x_ref[...]
    for step in range(count - 1):
        total = total + slots[step]
    o_ref[...] = total


def axis_sum(values, axis, collective_id):
    count = lax.axis_size(axis)
    if count == 1:
        return values
    return pl.pallas_call(
        functools.partial(axis_sum_kernel, axis, count),
        out_shape=jax.ShapeDtypeStruct(values.shape, values.dtype),
        in_specs=[pl.BlockSpec(memory_space=pltpu.VMEM)],
        out_specs=pl.BlockSpec(memory_space=pltpu.VMEM),
        scratch_shapes=[
            pltpu.VMEM((count - 1,) + values.shape, values.dtype),
            pltpu.SemaphoreType.DMA((count - 1,)),
            pltpu.SemaphoreType.DMA((count - 1,)),
        ],
        compiler_params=pltpu.CompilerParams(
            collective_id=collective_id, has_side_effects=True, vmem_limit_bytes=4 * 1024 * 1024
        ),
        name="axis_sum_" + axis,
    )(values)


LANES = 128
GROUP = 256


def normed_rows(widened, gain):
    center = widened - jnp.mean(widened, axis=-1, keepdims=True)
    spread = jnp.mean(center * center, axis=-1, keepdims=True)
    return (center * lax.rsqrt(spread + 1e-05) * gain).astype(jnp.bfloat16)


def mixer_kernel(
    layout, head_size, x_ref, gain_ref, bias_ref, late_gain_ref, proj_hbm, out_hbm, up_hbm, down_hbm,
    o_ref, triple, heads, proj_ref, out_w_ref, up_ref, down_ref, sems,
):
    kind, across = layout
    rows_total, feats = x_ref.shape
    tokens = WIN * WIN
    window_count = rows_total // tokens
    slabs = feats // LANES
    per_slab = LANES // head_size
    moves = [
        pltpu.make_async_copy(src, dst, sems.at[k])
        for k, (src, dst) in enumerate(
            ((proj_hbm, proj_ref), (out_hbm, out_w_ref), (up_hbm, up_ref), (down_hbm, down_ref))
        )
    ]
    moves[0].start()
    moves[0].wait()
    for move in moves[1:]:
        move.start()
    chunk = 256

    def project(step, carry):
        rows = pl.ds(pl.multiple_of(step * chunk, chunk), chunk)
        normed = normed_rows(x_ref[rows, :].astype(jnp.float32), gain_ref[...])
        for part in range(3 * slabs // 2):
            product = jnp.dot(
                normed, proj_ref[:, part * GROUP : (part + 1) * GROUP],
                preferred_element_type=jnp.float32,
            ).astype(jnp.bfloat16).astype(jnp.float32)
            triple[2 * part, rows, :] = product[:, :LANES]
            triple[2 * part + 1, rows, :] = product[:, LANES:]
        return carry

    lax.fori_loop(0, rows_total // chunk, project, 0)

    def places(window):
        if kind == "strided":
            return [pl.ds(window, tokens, stride=across)]
        per_row = across // WIN
        base = (window // per_row) * (WIN * across) + (window % per_row) * WIN
        return [pl.ds(pl.multiple_of(base + r * across, WIN), WIN) for r in range(WIN)]

    lane = lax.broadcasted_iota(jnp.int32, (tokens, GROUP), 1)
    head_of = (lane % LANES) // head_size
    scale = head_size ** (-0.5)

    def one_window(window):
        spots = places(window)

        def fetch(slab):
            pieces = [triple[slab, spot, :] for spot in spots]
            whole = pieces[0] if len(pieces) == 1 else jnp.concatenate(pieces, axis=0)
            return whole

        empty = jnp.zeros((tokens, LANES), jnp.bfloat16)
        for group in range(slabs // 2):
            first, second = 2 * group, 2 * group + 1
            query_0 = fetch(first).astype(jnp.bfloat16)
            query_1 = fetch(second).astype(jnp.bfloat16)
            keys = jnp.concatenate([fetch(slabs + first), fetch(slabs + second)], axis=1)
            vals = jnp.concatenate([fetch(2 * slabs + first), fetch(2 * slabs + second)], axis=1)
            block_q = jnp.concatenate(
                [
                    jnp.concatenate([query_0, empty], axis=1),
                    jnp.concatenate([empty, query_1], axis=1),
                ],
                axis=0,
            )
            block_k = jnp.concatenate(
                [jnp.where(head_of == j, keys, 0.0).astype(jnp.bfloat16) for j in range(per_slab)],
                axis=0,
            )
            block_v = jnp.concatenate(
                [jnp.where(head_of == j, vals, 0.0).astype(jnp.bfloat16) for j in range(per_slab)],
                axis=0,
            )
            scores = lax.dot_general(
                block_k, block_q, (((1,), (1,)), ((), ())), preferred_element_type=jnp.float32
            )
            scores = (scores * scale + bias_ref[group]).reshape(per_slab, tokens, 2 * tokens)
            weights = jnp.exp(scores - jnp.max(scores, axis=1, keepdims=True))
            shares = weights * (1.0 / jnp.sum(weights, axis=1, keepdims=True))
            shares = shares.reshape(per_slab * tokens, 2 * tokens).astype(jnp.bfloat16)
            mixed = lax.dot_general(
                shares, block_v, (((0,), (0,)), ((), ())), preferred_element_type=jnp.float32
            )
            for slab, part in (
                (first, mixed[:tokens, :LANES]), (second, mixed[tokens:, LANES:])
            ):
                if len(spots) == 1:
                    heads[slab, spots[0], :] = part
                else:
                    for r, spot in enumerate(spots):
                        heads[slab, spot, :] = part[r * WIN : (r + 1) * WIN]

    def attend_pair(step, carry):
        one_window(2 * step)
        one_window(2 * step + 1)
        return carry

    lax.fori_loop(0, window_count // 2, attend_pair, 0)
    for move in moves[1:]:
        move.wait()
    hidden_width = up_ref.shape[1]
    tile = 512

    def feed(step, carry):
        rows = pl.ds(pl.multiple_of(step * chunk, chunk), chunk)
        mixed = jnp.concatenate([heads[s, rows, :] for s in range(slabs)], axis=1).astype(jnp.bfloat16)
        value = (
            x_ref[rows, :].astype(jnp.float32)
            + jnp.dot(mixed, out_w_ref[...], preferred_element_type=jnp.float32)
        ).astype(jnp.bfloat16).astype(jnp.float32)
        normed = normed_rows(value, late_gain_ref[...])
        for k in range(hidden_width // tile):
            part = slice(k * tile, (k + 1) * tile)
            hidden = jax.nn.gelu(
                jnp.dot(normed, up_ref[:, part], preferred_element_type=jnp.float32),
                approximate=True,
            ).astype(jnp.bfloat16)
            value = value + jnp.dot(hidden, down_ref[part, :], preferred_element_type=jnp.float32)
        o_ref[rows, :] = value.astype(jnp.bfloat16)
        return carry

    lax.fori_loop(0, rows_total // chunk, feed, 0)


def mixer(x, layout, gain, in_weight, out_weight, bias, late_gain, up, down, heads_count):
    rows, feats = x.shape
    vmem = pl.BlockSpec(memory_space=pltpu.VMEM)
    hbm = pl.BlockSpec(memory_space=pltpu.HBM)
    flops = 8 * rows * feats * (4 * feats + 2 * up.shape[1])
    return pl.pallas_call(
        functools.partial(mixer_kernel, layout, feats // heads_count),
        out_shape=jax.ShapeDtypeStruct((rows, feats), jnp.bfloat16),
        in_specs=[vmem] * 4 + [hbm] * 4,
        out_specs=vmem,
        scratch_shapes=[
            pltpu.VMEM((3 * feats // LANES, rows, LANES), jnp.float32),
            pltpu.VMEM((feats // LANES, rows, LANES), jnp.float32),
            pltpu.VMEM(in_weight.shape, jnp.bfloat16),
            pltpu.VMEM(out_weight.shape, jnp.bfloat16),
            pltpu.VMEM(up.shape, jnp.bfloat16),
            pltpu.VMEM(down.shape, jnp.bfloat16),
            pltpu.SemaphoreType.DMA((4,)),
        ],
        compiler_params=pltpu.CompilerParams(vmem_limit_bytes=60 * 1024 * 1024),
        cost_estimate=pl.CostEstimate(
            flops=flops, bytes_accessed=12 * 1024 * 1024, transcendentals=0
        ),
        name="mixer_" + layout[0],
    )(x, gain[None], bias, late_gain[None], in_weight, out_weight, up, down)


def key_major_bias(table, down, across):
    head_count, spots = table.shape
    relative = (down[None, :] - down[:, None] + WIN - 1) * (2 * WIN - 1) + (
        across[None, :] - across[:, None] + WIN - 1
    )
    tokens = WIN * WIN
    chosen = (jnp.arange(spots)[:, None] == jnp.asarray(relative.reshape(-1))[None, :]).astype(
        jnp.float32
    )
    spread = jnp.dot(table, chosen, precision=lax.Precision.HIGHEST)
    return (
        spread.reshape(head_count // 8, 2, 4, tokens, tokens)
        .transpose(0, 2, 3, 1, 4)
        .reshape(head_count // 8, 4 * tokens, 2 * tokens)
    )


def split_sublayers(conv_out, run_block, run_grid, block_table, grid_table):
    row_devices = lax.axis_size("row")
    col_devices = lax.axis_size("col")
    row_count, col_count, feats = conv_out.shape
    plain = np.arange(WIN * WIN)
    block_bias = key_major_bias(block_table, plain // WIN, plain % WIN)
    if row_devices > WIN or col_devices > WIN:
        section = run_block(conv_out.reshape(-1, feats), ("blocks", col_count), block_bias)
        windows = grid_layout(section.reshape(row_count, col_count, feats))
        count = windows.shape[0]
        bias = key_major_bias(grid_table, plain // WIN, plain % WIN)
        out = run_grid(windows.transpose(1, 0, 2).reshape(-1, feats), ("strided", count), bias)
        out = out.reshape(WIN * WIN, count, feats).transpose(1, 0, 2)
        return spatial_layout(out, row_count, col_count)
    devices = row_devices * col_devices
    row_fold, col_fold = WIN // row_devices, WIN // col_devices
    row_rest, col_rest = row_count // row_fold, col_count // col_fold
    parts = row_rest // WIN
    count = WIN * col_rest // devices
    pieces = col_rest // count
    order = np.arange(WIN * WIN).reshape(row_devices, col_devices, row_fold, col_fold)
    at = np.indices(order.shape).reshape(4, -1)
    grid_bias = key_major_bias(grid_table, at[0] * row_fold + at[2], at[1] * col_fold + at[3])
    strips = conv_out.reshape(row_fold, parts, WIN, col_count, feats)
    results = []
    for part in range(parts):
        section = run_block(
            strips[:, part].reshape(-1, feats), ("blocks", col_count), block_bias
        )
        sent = (
            section.reshape(row_fold, WIN, col_fold, pieces, count, feats)
            .transpose(1, 3, 0, 2, 4, 5)
            .reshape(devices, row_fold * col_fold * count, feats)
        )
        got = lax.all_to_all(sent, ("row", "col"), split_axis=0, concat_axis=0, tiled=True)
        out = run_grid(got.reshape(-1, feats), ("strided", count), grid_bias)
        back = lax.all_to_all(
            out.reshape(devices, -1, feats), ("row", "col"), split_axis=0, concat_axis=0, tiled=True
        )
        results.append(
            back.reshape(WIN, pieces, row_fold, col_fold, count, feats)
            .transpose(2, 0, 3, 1, 4, 5)
            .reshape(row_fold, WIN, col_count, feats)
        )
    return jnp.stack(results, axis=1).reshape(row_count, col_count, feats)


PAD = 8


def conv_kernel(
    row_count, col_count, flags, ext_ref, scale_ref, shift_ref, expand_ref, taps_ref,
    o_ref, sums_ref, conv_in, expanded,
):
    wide = col_count + PAD
    tall = row_count + 2
    width = expand_ref.shape[1]
    block = expanded.shape[-1]
    bounds = [8 * k for k in range(row_count // 8)] + [tall]
    for low, high in zip(bounds[:-1], bounds[1:]):
        rows = slice(low * wide, high * wide)
        conv_in[rows, :] = (
            ext_ref[rows, :].astype(jnp.float32) * scale_ref[...] + shift_ref[...]
        ).astype(jnp.bfloat16)
    spot = lax.broadcasted_iota(jnp.int32, (1, PAD, block), 1)
    side = jnp.where(spot == 0, flags[3], jnp.where(spot == PAD - 1, flags[2], 0.0))

    def channels(step, carry):
        lanes = pl.ds(pl.multiple_of(step * block, block), block)
        for low, high in zip(bounds[:-1], bounds[1:]):
            product = jnp.dot(
                conv_in[low * wide : high * wide, :], expand_ref[:, lanes],
                preferred_element_type=jnp.float32,
            )
            value = jax.nn.gelu(product, approximate=True).astype(jnp.bfloat16)
            expanded[low:high] = value.astype(jnp.float32).reshape(high - low, wide, block)
        expanded[0] = expanded[0] * flags[0]
        expanded[tall - 1] = expanded[tall - 1] * flags[1]
        expanded[:, col_count:, :] = expanded[:, col_count:, :] * side
        for half in range(block // LANES):
            inner = slice(half * LANES, (half + 1) * LANES)
            outer = pl.ds(pl.multiple_of(step * block + half * LANES, LANES), LANES)
            taps = [taps_ref[k : k + 1, outer] for k in range(9)]

            def rows_of(group, total):
                base = group * 4
                held = [expanded[base + k, :, inner] for k in range(6)]
                for k in range(4):
                    parts = [
                        held[k] * taps[side_step]
                        + held[k + 1] * taps[3 + side_step]
                        + held[k + 2] * taps[6 + side_step]
                        for side_step in range(3)
                    ]
                    summed = (
                        pltpu.roll(parts[0], 1, 0) + parts[1] + pltpu.roll(parts[2], wide - 1, 0)
                    )[:col_count]
                    deep = jax.nn.gelu(summed, approximate=True)
                    total = total + jnp.sum(deep.reshape(col_count // 8, 8, LANES), axis=0)
                    at = pl.ds(pl.multiple_of((base + k) * col_count, col_count), col_count)
                    o_ref[at, outer] = deep.astype(o_ref.dtype)
                return total

            total = lax.fori_loop(0, row_count // 4, rows_of, jnp.zeros((8, LANES), jnp.float32))
            sums_ref[:, outer] = jnp.sum(total, axis=0, keepdims=True)
        return carry

    lax.fori_loop(0, width // block, channels, 0)


def depthwise_stage(latent, conv_scale, conv_shift, expand_weight, depth_kernel):
    row_count, col_count, feats = latent.shape
    width = expand_weight.shape[1]
    row_at, col_at = lax.axis_index("row"), lax.axis_index("col")
    flags = jnp.stack(
        [row_at > 0, row_at < lax.axis_size("row") - 1, col_at > 0, col_at < lax.axis_size("col") - 1]
    ).astype(jnp.float32)
    tall = extended(latent, (("row", 0),), 1)
    count = lax.axis_size("col")
    ahead = [(i, i + 1) for i in range(count - 1)]
    left = lax.ppermute(tall[:, col_count - 1 :], "col", ahead)
    right = lax.ppermute(tall[:, :1], "col", [(b, a) for a, b in ahead])
    blank = jnp.zeros((row_count + 2, PAD - 2, feats), latent.dtype)
    ext = jnp.concatenate([tall, right, blank, left], axis=1).reshape(-1, feats)
    vmem = pl.BlockSpec(memory_space=pltpu.VMEM)
    block = 256
    return pl.pallas_call(
        functools.partial(conv_kernel, row_count, col_count),
        out_shape=(
            jax.ShapeDtypeStruct((row_count * col_count, width), jnp.bfloat16),
            jax.ShapeDtypeStruct((1, width), jnp.float32),
        ),
        in_specs=[pl.BlockSpec(memory_space=pltpu.SMEM)] + [vmem] * 5,
        out_specs=(vmem, vmem),
        scratch_shapes=[
            pltpu.VMEM(ext.shape, jnp.bfloat16),
            pltpu.VMEM((row_count + 2, col_count + PAD, block), jnp.float32),
        ],
        compiler_params=pltpu.CompilerParams(vmem_limit_bytes=20 * 1024 * 1024),
        name="conv_stage",
    )(flags, ext, conv_scale[None], conv_shift[None], expand_weight, depth_kernel)


def per_device(
    latent,
    conv_scale,
    conv_shift,
    expand_weight,
    depth_kernel,
    squeeze_down,
    squeeze_up,
    project_weight,
    block_gain,
    block_projection,
    block_output,
    block_table,
    first_gain,
    first_expand,
    first_reduce,
    grid_gain,
    grid_projection,
    grid_output,
    grid_table,
    second_gain,
    second_expand,
    second_reduce,
):
    row_devices = lax.axis_size("row")
    col_devices = lax.axis_size("col")
    row_count, col_count, channels = latent.shape
    depthwise, local_sums = depthwise_stage(
        latent, conv_scale, conv_shift, expand_weight, depth_kernel
    )
    local_sums = local_sums.reshape(-1, LANES)
    channel_sums = axis_sum(axis_sum(local_sums, "row", 1), "col", 2).reshape(-1)
    pooled = channel_sums / (row_count * row_devices * col_count * col_devices)
    excite = squeeze_gate(pooled, squeeze_down, squeeze_up)
    gated = (depthwise.astype(jnp.float32) * excite).astype(jnp.bfloat16)
    conv_out = (
        latent.reshape(-1, channels).astype(jnp.float32)
        + jnp.dot(gated, project_weight, preferred_element_type=jnp.float32)
    ).astype(jnp.bfloat16).reshape(row_count, col_count, channels)

    def run_block(cells, layout, bias):
        return mixer(
            cells, layout, block_gain, block_projection, block_output, bias, first_gain,
            first_expand, first_reduce, block_table.shape[0],
        )

    def run_grid(cells, layout, bias):
        return mixer(
            cells, layout, grid_gain, grid_projection, grid_output, bias, second_gain,
            second_expand, second_reduce, grid_table.shape[0],
        )

    return split_sublayers(conv_out, run_block, run_grid, block_table, grid_table)


def solution(mesh):
    placed = (
        P("row", "col", None),
        P(),
        P(),
        P(),
        P(),
        P(),
        P(),
        P(),
        P(),
        P(),
        P(),
        P(),
        P(),
        P(),
        P(),
        P(),
        P(),
        P(),
        P(),
        P(),
        P(),
        P(),
    )
    return jax.shard_map(
        per_device, mesh=mesh, in_specs=placed, out_specs=P("row", "col", None), check_vma=False
    )
```
